32 devices in a mesh: qrow: 8 (over z, x), kcol: 4 (over y, core).
Axes of the slice: x: 2, y: 2, z: 4, core: 2. Of those that a mesh axis runs over, the one named last changes fastest.
Arguments:
- queries: bfloat16 [128, 8192], P(('qrow', 'kcol')), may hold values from -200 to 200
- keys_values: bfloat16 [2, 4096, 512], P(None, ('kcol', 'qrow')), may hold values from -8 to 8
- doc_blocks: int32 [32], replicated, may hold values from 0 to 1, never falling along the last dimension, each value on 1 to 17 neighbouring positions
Outputs:
- attended: bfloat16 [128, 8192], P(('qrow', 'kcol'))
The draws below stay inside these ranges and needn't reach their ends.
Inputs may be any that keep to these rules, and one draw needn't show every extreme that they name: doc_blocks[b] is the document of positions 128 b to 128 b + 127; each document covers 1 to 17 consecutive entries (blocks), one document exactly that many.
All inputs are finite; a program needn't handle non-finite values.
Results may differ from the reference program's by a relative error of at most 0.0046.
Values may be sent and summed in bfloat16 or wider, within the bound.
A program may use at most 128 MiB of HBM per device.

```python
import math
import jax
import jax.numpy as jnp
import numpy as np
from jax import lax

QUERY_HEADS = 64
KEY_VALUE_HEADS = 4
HEAD_WIDTH = 128
TQ = 128
TOTAL_KEY_COUNT = 4096
STRIPE = 4096
KBLK = 32
DOCS = 2
N_KCOL = 4


def base_keys(key):
    return jax.random.truncated_normal(jax.random.fold_in(key, 11), -6.0, 6.0, (TOTAL_KEY_COUNT, KEY_VALUE_HEADS * HEAD_WIDTH), jnp.float32)


def draw_queries(key, part):
    shape_all = (TQ, QUERY_HEADS * HEAD_WIDTH)
    return jax.random.truncated_normal(jax.random.fold_in(key, 23), -6.0, 6.0, shape_all, jnp.float32).astype(jnp.bfloat16)


def draw_keys_values(key, part):
    key_matrix_rows = base_keys(key)
    value_matrix_rows = jax.random.truncated_normal(jax.random.fold_in(key, 37), -6.0, 6.0, (TOTAL_KEY_COUNT, KEY_VALUE_HEADS * HEAD_WIDTH), jnp.float32)
    return jnp.stack([key_matrix_rows, value_matrix_rows]).astype(jnp.bfloat16)


def split_up(amount, total, reach, slope):
    loads = [(1 << 20) // math.isqrt(grade ** slope) + 1 for grade in range(2, amount + 1)]
    surplus, counts = total - reach - (amount - 1), [1] * (amount - 1)
    while surplus > 0:
        candidates = [i for i in range(amount - 1) if counts[i] < reach]
        whole, left = sum([loads[i] for i in candidates]), surplus
        for i in candidates:
            addition = min(reach - counts[i], max(1, left * loads[i] // whole), surplus)
            counts[i] = counts[i] + addition
            surplus = surplus - addition
    return np.array([reach] + counts)


def ragged(own_key, amount, total, most, lean):
    if amount == 2:
        one = jax.random.randint(own_key, (), max(1, total - most), min(most, total - 1) + 1)
        return jnp.stack([one, total - one])
    tallies = jnp.asarray(split_up(amount, total, most, lean), jnp.int32)
    pairs = (amount - 1) // 2
    giver, sink = tallies[1:1 + 2 * pairs:2], tallies[2:2 + 2 * pairs:2]
    margin = jnp.minimum(giver - 1, most - sink)
    moved = jax.random.randint(jax.random.fold_in(own_key, 1), (pairs,), 0, 1 << 20) % (margin + 1)
    tallies = tallies.at[1:1 + 2 * pairs:2].set(giver - moved).at[2:2 + 2 * pairs:2].set(sink + moved)
    return tallies[jax.random.permutation(jax.random.fold_in(own_key, 2), amount)]


def setup_inputs(seed: int = 0) -> dict:
    key_of = jax.random.split(jax.random.key(seed), 4)
    queries = draw_queries(jax.random.fold_in(key_of[3], 71), 0)
    keys_values = draw_keys_values(jax.random.fold_in(key_of[3], 71), 0)
    doc_blocks = jnp.searchsorted(jnp.cumsum(ragged(key_of[2], DOCS, KBLK, KBLK // 2 + 1, 2)), jnp.arange(KBLK), side="right").astype(jnp.int32)
    return {"queries": queries, "keys_values": keys_values, "doc_blocks": doc_blocks}


masked_score = -1e+30

def reference(queries, keys_values, doc_blocks):
    query_group_width = QUERY_HEADS // KEY_VALUE_HEADS
    range_keys = TOTAL_KEY_COUNT // N_KCOL
    score_scale = 1.0 / math.sqrt(HEAD_WIDTH)
    key_pos = jnp.arange(TOTAL_KEY_COUNT, dtype=jnp.int32)
    key_doc = jnp.repeat(doc_blocks, 128)
    key_matrix_rows = keys_values[0].astype(jnp.float32)
    value_matrix_rows = keys_values[1].astype(jnp.float32)

    def one_block(block_index):
        block_index = block_index.astype(jnp.int32)
        first_row = block_index * 128
        query_rows = lax.dynamic_slice_in_dim(queries, first_row, 128, 0).astype(jnp.float32)
        query_pos = block_index * STRIPE + STRIPE - 128 + jnp.arange(128, dtype=jnp.int32)
        query_doc = doc_blocks[block_index * (STRIPE // 128) + STRIPE // 128 - 1]
        live_mask = (key_doc[None, :] == query_doc) & (key_pos[None, :] <= query_pos[:, None])
        ranged_mask = live_mask.reshape(1, 128, N_KCOL, range_keys)
        head_outputs = []
        for query_head_group in range(KEY_VALUE_HEADS):
            grouped = query_rows[:, query_head_group * query_group_width * HEAD_WIDTH:(query_head_group + 1) * query_group_width * HEAD_WIDTH].reshape(128, query_group_width, HEAD_WIDTH)
            key_part = key_matrix_rows[:, query_head_group * HEAD_WIDTH:(query_head_group + 1) * HEAD_WIDTH]
            value_part = value_matrix_rows[:, query_head_group * HEAD_WIDTH:(query_head_group + 1) * HEAD_WIDTH].reshape(N_KCOL, range_keys, HEAD_WIDTH)
            scores = jnp.einsum('qhd,kd->hqk', grouped, key_part) * score_scale
            scores = jnp.where(live_mask[None], scores, masked_score).reshape(query_group_width, 128, N_KCOL, range_keys)
            range_max = lax.optimization_barrier(jnp.max(scores, axis=3))
            weights = jnp.where(ranged_mask, jnp.exp(scores - range_max[..., None]), 0.0)
            range_sum = lax.optimization_barrier(jnp.sum(weights, axis=3))
            rounded = lax.optimization_barrier(weights.astype(jnp.bfloat16)).astype(jnp.float32)
            range_out = jnp.einsum('hqrk,rkd->hqrd', rounded, value_part)
            overall = lax.optimization_barrier(jnp.max(range_max, axis=2))
            factor = jnp.exp(range_max - overall[..., None])
            total_out = lax.optimization_barrier(jnp.sum(range_out * factor[..., None], axis=2))
            total_sum = lax.optimization_barrier(jnp.sum(range_sum * factor, axis=2))
            head_outputs.append(total_out / total_sum[..., None])
        joined = jnp.concatenate(head_outputs, axis=0)
        return jnp.transpose(joined, (1, 0, 2)).reshape(128, QUERY_HEADS * HEAD_WIDTH).astype(jnp.bfloat16)
    blocks = lax.map(one_block, jnp.arange(TQ // 128, dtype=jnp.int32))
    return blocks.reshape(TQ, QUERY_HEADS * HEAD_WIDTH)
```

```python
import math

import jax
import jax.numpy as jnp
from jax import lax
from jax.experimental import pallas as pl
from jax.experimental.pallas import tpu as pltpu
from jax.sharding import PartitionSpec as P

QUERY_HEADS = 64
KEY_VALUE_HEADS = 4
HEAD_WIDTH = 128
BLOCK = 128
MESH = pl.DeviceIdType.MESH

masked_score = -1e30


def dot(a, b, dims):
    return lax.dot_general(a, b, (dims, ((), ())), preferred_element_type=jnp.float32)


def make_kernel(rows_n, cols_n, local_rows, blocks_n):
    fold = max(1, 8 // cols_n)
    groups = rows_n // fold
    members = fold * cols_n
    heads = QUERY_HEADS // members
    slice_rows = local_rows * heads
    chunk_rows = members * slice_rows
    devices = rows_n * cols_n
    total_queries = devices * local_rows
    query_blocks = total_queries // BLOCK
    stripe_blocks = blocks_n // query_blocks
    chunk_queries = members * local_rows
    assert BLOCK % chunk_queries == 0 and blocks_n == devices and cols_n % 2 == 0 and 2 * slice_rows <= BLOCK
    first_live = max(0, stripe_blocks - 1 - blocks_n // 2)
    block_of = lambda e, g: (e % cols_n) * rows_n + g * fold + e // cols_n
    spans = [[block_of(e, g) >= first_live for g in range(groups)] for e in range(members)]
    sure = [e for e in range(members) if all(spans[e])]
    maybe = [e for e in range(members) if any(spans[e]) and not all(spans[e])]
    slots = sure + maybe
    scale = math.log2(math.e) / math.sqrt(HEAD_WIDTH)

    apart = max(1, groups // 2)

    def visited(group, k):
        block = group // apart
        far = lax.rem(block + 1, groups // apart) * apart + lax.rem(group + k, apart)
        near = block * apart + lax.rem(group + k - apart, apart)
        return jnp.where(k == 0, group, jnp.where(k <= apart, far, near))

    def where_is(group, member):
        return (group * fold + member // cols_n, member % cols_n)

    def kernel(doc_any, q_any, kv_ref, out_ref, doc_ref, q_ref, in_sems, local, local_sem, qsend, wide, qbuf, kvbuf, osend, ssend, obuf, sbuf,
               q_send, q_recv, kv_send, kv_recv, pair_send, pair_recv, o_send, o_recv, s_send, s_recv):
        row, col = lax.axis_index("qrow"), lax.axis_index("kcol")
        group = row // fold
        member = (row % fold) * cols_n + col
        me = row * cols_n + col
        my_block = col * rows_n + row
        my_slot = sum(i * (member == e).astype(jnp.int32) for i, e in enumerate(slots))

        half = lax.rem(member, 2)
        barrier = pltpu.get_barrier_semaphore()

        @pl.loop(1, devices)
        def _(k):
            other = lax.rem(me + k, devices)
            pl.semaphore_signal(barrier, inc=1, device_id=(other // cols_n, other % cols_n), device_id_type=MESH)

        q_fetch = pltpu.make_async_copy(q_any, q_ref, in_sems.at[0])
        q_fetch.start()
        doc_fetch = pltpu.make_async_copy(doc_any, doc_ref, in_sems.at[1])
        doc_fetch.start()
        fetch = pltpu.make_async_copy(kv_ref, local, local_sem)
        fetch.start()

        for i, e in enumerate(maybe):
            @pl.when(block_of(e, group) < first_live)
            def _():
                kvbuf[:, len(sure) + i] = jnp.zeros((2, BLOCK, HEAD_WIDTH), kvbuf.dtype)

        q_fetch.wait()
        doc_fetch.wait()
        for e in range(members):
            for h in range(heads):
                first = (e * heads + h) * HEAD_WIDTH
                wide[e, h * local_rows:(h + 1) * local_rows] = q_ref[:, first:first + HEAD_WIDTH].astype(jnp.float32)
            qsend[e] = wide[e].astype(qsend.dtype)

        fetch.wait()
        pl.semaphore_wait(barrier, devices - 1)

        def kv_part(e):
            first = pl.multiple_of(e * heads // (QUERY_HEADS // KEY_VALUE_HEADS) * HEAD_WIDTH, HEAD_WIDTH)
            return local.at[lax.rem(e, 2), :, pl.ds(first, HEAD_WIDTH)]

        def kv_copy(k):
            e = lax.rem(member + k, members)
            return pltpu.make_async_remote_copy(
                src_ref=kv_part(e), dst_ref=kvbuf.at[lax.rem(e, 2), my_slot], send_sem=kv_send.at[k],
                recv_sem=kv_recv.at[my_slot], device_id=where_is(group, e), device_id_type=MESH)

        @pl.when(my_block >= first_live)
        def _():
            pltpu.make_async_copy(kv_part(member), kvbuf.at[half, my_slot], kv_recv.at[my_slot]).start()
            for k in range(1, members):
                kv_copy(k).start()

        pltpu.make_async_copy(qsend.at[member], qbuf.at[me], q_recv.at[group]).start()

        @pl.loop(1, devices)
        def _(k):
            e = lax.rem(member + k, members)
            pltpu.make_async_remote_copy(
                src_ref=qsend.at[e], dst_ref=qbuf.at[me], send_sem=q_send, recv_sem=q_recv.at[group],
                device_id=where_is(visited(group, k // members), e), device_id_type=MESH).start()

        def pair_copy(i):
            return pltpu.make_async_remote_copy(
                src_ref=kvbuf.at[half, i], dst_ref=kvbuf.at[half, i], send_sem=pair_send.at[i],
                recv_sem=pair_recv.at[i], device_id=(row, col + 1 - 2 * lax.rem(col, 2)), device_id_type=MESH)

        def per_slot(step):
            for i, e in enumerate(slots):
                if e in sure:
                    step(i)
                else:
                    pl.when(block_of(e, group) >= first_live)(lambda: step(i))

        def pass_on(i):
            pltpu.make_async_copy(kvbuf.at[half, i], kvbuf.at[half, i], kv_recv.at[i]).wait()
            pair_copy(i).start()

        per_slot(pass_on)
        per_slot(lambda i: pair_copy(i).wait_recv())

        lane = lax.broadcasted_iota(jnp.int32, (chunk_rows, BLOCK), 1)
        row_index = lax.broadcasted_iota(jnp.int32, (chunk_rows, BLOCK), 0)
        row_query = row_index // slice_rows * local_rows + row_index % local_rows
        offset = (lax.broadcasted_iota(jnp.int32, (slice_rows, BLOCK), 1)
                  - lax.broadcasted_iota(jnp.int32, (slice_rows, BLOCK), 0))
        top_place, total_place = offset == 0, offset == slice_rows

        def attend(source):
            first = source * members
            mine = qbuf.at[pl.ds(first, members)]
            pltpu.make_async_copy(mine, mine, q_recv.at[source]).wait()
            q = qbuf[pl.ds(first, members)].reshape(chunk_rows, HEAD_WIDTH)
            query_first = source * chunk_queries
            query_block = (query_first // BLOCK + 1) * stripe_blocks - 1
            in_block = row_query + query_first % BLOCK
            query_doc = doc_ref[query_block]
            keys = kvbuf[0].reshape(len(slots) * BLOCK, HEAD_WIDTH)
            values = kvbuf[1].reshape(len(slots) * BLOCK, HEAD_WIDTH)
            scores = dot(q, keys, ((1,), (1,)))
            masked = []
            for i, e in enumerate(slots):
                b = block_of(e, group)
                same = doc_ref[b] == query_doc
                whole = jnp.where(same & (b < query_block), BLOCK, -1)
                causal = jnp.where(same & (b == query_block), 0, -2 * BLOCK)
                limit = jnp.maximum(in_block + causal, whole)
                masked.append(jnp.where(lane <= limit, scores[:, i * BLOCK:(i + 1) * BLOCK], masked_score))
            top = masked[0]
            for s in masked[1:]:
                top = jnp.maximum(top, s)
            top = jnp.maximum(jnp.max(top, axis=1, keepdims=True), 0.5 * masked_score)
            weights = [jnp.exp2((s - top) * scale) for s in masked]
            total = weights[0]
            for p in weights[1:]:
                total = total + p
            total = jnp.sum(total, axis=1, keepdims=True)
            acc = dot(jnp.concatenate([p.astype(jnp.bfloat16) for p in weights], axis=1), values, ((1,), (0,)))
            osend[pl.ds(first, members)] = acc.astype(jnp.bfloat16).reshape(members, slice_rows, HEAD_WIDTH)
            for j in range(members):
                part = slice(j * slice_rows, (j + 1) * slice_rows)
                stats = jnp.where(top_place, top[part], jnp.where(total_place, total[part], 0.0))
                ssend[first + j] = jnp.sum(stats, axis=0, keepdims=True)

        def give(source, j):
            k = source * members + j
            return [
                pltpu.make_async_remote_copy(
                    src_ref=src.at[k], dst_ref=dst.at[group, member], send_sem=sent, recv_sem=got.at[group],
                    device_id=where_is(source, j), device_id_type=MESH)
                for src, dst, sent, got in ((osend, obuf, o_send, o_recv), (ssend, sbuf, s_send, s_recv))
            ]

        def step(k):
            source = lax.rem(group + k, groups)
            attend(source)
            for j in range(members):
                for copy in give(source, j):
                    copy.start()

        if groups <= 4:
            for k in range(1, groups):
                step(k)
        else:
            pl.loop(1, groups)(step)

        attend(group)
        pltpu.make_async_copy(osend.at[me], obuf.at[group, member], o_recv.at[group]).start()
        pltpu.make_async_copy(ssend.at[me], sbuf.at[group, member], s_recv.at[group]).start()
        for i in range(1, members):
            for copy in give(group, lax.rem(member + i, members)):
                copy.start()

        for g in range(groups):
          pltpu.make_async_copy(sbuf.at[g], sbuf.at[g], s_recv.at[g]).wait()
          pltpu.make_async_copy(obuf.at[g], obuf.at[g], o_recv.at[g]).wait()

        for e in range(members):
            column = lambda g, place: jnp.sum(jnp.where(place, sbuf[g, e], 0.0), axis=1, keepdims=True)
            tops = [column(g, top_place) for g in range(groups)]
            overall = tops[0]
            for t in tops[1:]:
                overall = jnp.maximum(overall, t)
            merged = weight = None
            for g in range(groups):
                factor = jnp.exp2((tops[g] - overall) * scale)
                term = factor * obuf[g, e].astype(jnp.float32)
                part = factor * column(g, total_place)
                merged = term if merged is None else merged + term
                weight = part if weight is None else weight + part
            wide[e] = merged / weight
            for h in range(heads):
                first = (e * heads + h) * HEAD_WIDTH
                out_ref[:, first:first + HEAD_WIDTH] = wide[e, h * local_rows:(h + 1) * local_rows].astype(out_ref.dtype)

        per_slot(lambda i: pair_copy(i).wait_send())

        @pl.when(my_block >= first_live)
        def _():
            for k in range(1, members):
                kv_copy(k).wait_send()
        others = qbuf.at[pl.ds(0, devices - 1)]
        pltpu.make_async_copy(others, others, q_send).wait()
        others = osend.at[pl.ds(0, devices - 1)]
        pltpu.make_async_copy(others, others, o_send).wait()
        others = ssend.at[pl.ds(0, devices - 1)]
        pltpu.make_async_copy(others, others, s_send).wait()

    bf16, dma = jnp.bfloat16, pltpu.SemaphoreType.DMA
    scratch = [
        pltpu.SMEM((blocks_n,), jnp.int32),
        pltpu.VMEM((local_rows, QUERY_HEADS * HEAD_WIDTH), jnp.bfloat16),
        pltpu.SemaphoreType.DMA((2,)),
        pltpu.VMEM((2, BLOCK, KEY_VALUE_HEADS * HEAD_WIDTH), bf16),
        dma,
        pltpu.VMEM((members, slice_rows, HEAD_WIDTH), bf16),
        pltpu.VMEM((members, slice_rows, HEAD_WIDTH), jnp.float32),
        pltpu.VMEM((devices, slice_rows, HEAD_WIDTH), bf16),
        pltpu.VMEM((2, len(slots), BLOCK, HEAD_WIDTH), bf16),
        pltpu.VMEM((devices, slice_rows, HEAD_WIDTH), bf16),
        pltpu.VMEM((devices, 1, BLOCK), jnp.float32),
        pltpu.VMEM((groups, members, slice_rows, HEAD_WIDTH), bf16),
        pltpu.VMEM((groups, members, 1, BLOCK), jnp.float32),
        dma, dma((groups,)), dma((members,)), dma((len(slots),)), dma((len(slots),)), dma((len(slots),)),
        dma, dma((groups,)), dma, dma((groups,)),
    ]
    return kernel, scratch


def solution(mesh):
    rows_n, cols_n = mesh.shape["qrow"], mesh.shape["kcol"]

    def per_device(queries, keys_values, doc_blocks):
        local_rows = queries.shape[0]
        kernel, scratch = make_kernel(rows_n, cols_n, queries.shape[0], doc_blocks.shape[0])
        merged = pl.pallas_call(
            kernel,
            out_shape=pltpu.VMEM(queries.shape, queries.dtype),
            in_specs=[
                pl.BlockSpec(memory_space=pl.ANY),
                pl.BlockSpec(memory_space=pl.ANY),
                pl.BlockSpec(memory_space=pl.ANY),
            ],
            out_specs=pl.BlockSpec(memory_space=pltpu.VMEM),
            scratch_shapes=scratch,
            compiler_params=pltpu.CompilerParams(collective_id=0, has_side_effects=True),
        )(doc_blocks, queries, keys_values)

        return merged

    return jax.shard_map(
        per_device,
        mesh=mesh,
        in_specs=(P(("qrow", "kcol"), None), P(None, ("kcol", "qrow"), None), P()),
        out_specs=P(("qrow", "kcol"), None),
        check_vma=False,
    )
```

```python
import math

import jax
import jax.numpy as jnp
from jax import lax
from jax.experimental import pallas as pl
from jax.experimental.pallas import tpu as pltpu
from jax.sharding import PartitionSpec as P

QUERY_HEADS = 64
KEY_VALUE_HEADS = 4
HEAD_WIDTH = 128
BLOCK = 128
MESH = pl.DeviceIdType.MESH

masked_score = -1e30


def dot(a, b, dims):
    return lax.dot_general(a, b, (dims, ((), ())), preferred_element_type=jnp.float32)


def make_kernel(rows_n, cols_n, local_rows, blocks_n):
    fold = max(1, 8 // cols_n)
    planes = rows_n // fold
    members = fold * cols_n
    chips = members // 2
    classes = planes // 2
    heads = QUERY_HEADS // members
    slice_rows = local_rows * heads
    chunk_rows = members * slice_rows
    devices = rows_n * cols_n
    total_queries = devices * local_rows
    query_blocks = total_queries // BLOCK
    stripe_blocks = blocks_n // query_blocks
    chunk_queries = members * local_rows
    messages = classes * members
    assert BLOCK % chunk_queries == 0 and blocks_n == devices and cols_n % 2 == 0 and 2 * slice_rows <= BLOCK
    assert planes % 2 == 0
    first_live = max(0, stripe_blocks - 1 - blocks_n // 2)
    block_of = lambda e, p: (e % cols_n) * rows_n + p * fold + e // cols_n
    alive = lambda e, half: [block_of(e, p) >= first_live for p in range(half, planes, 2)]
    sure = [e for e in range(members) if all(alive(e, 0) + alive(e, 1))]
    maybe = [(half, e) for half in range(2) for e in range(members) if e not in sure and any(alive(e, half))]
    spare = 2 * len(sure)
    slots_n = spare + len(maybe)
    scale = math.log2(math.e) / math.sqrt(HEAD_WIDTH)

    assert sure and chips & (chips - 1) == 0
    steps = sorted(range(1, chips), key=lambda k: (bin(k).count("1"), -k))

    def crossed(chip, k):
        bits = [1 << n for n in range(chips.bit_length() - 1) if k >> n & 1]
        return chip + sum(bit * (1 - 2 * (chip // bit % 2)) for bit in bits)

    def where_is(plane, member):
        return (plane * fold + member // cols_n, member % cols_n)

    def kernel(doc_any, q_any, kv_any, out_ref, doc_ref, q_ref, local, in_sems, plane_sem, cross_sem,
               qsend, wide, qbuf, kvbuf, early_top, early_total, early_acc, osend, ssend, obuf, sbuf,
               q_send, q_recv, kv_send, kv_recv, pass_send, relay_send, o_send, o_recv, s_send, s_recv):
        row, col = lax.axis_index("qrow"), lax.axis_index("kcol")
        plane, core = row // fold, lax.rem(col, 2)
        member = (row % fold) * cols_n + col
        chip = member // 2
        half, kind = lax.rem(plane, 2), plane // 2
        mate = plane + 1 - 2 * half
        me = kind * members + member
        my_block = block_of(member, plane)
        partner = (row, col + 1 - 2 * core)
        mate_core = where_is(mate, chip * 2 + 1)
        is_first, is_second = core == 0, core == 1
        barrier = pltpu.get_barrier_semaphore()

        def peer_plane(k):
            return lax.rem(kind + k, classes) * 2 + half

        def greet(plane_, member_):
            pl.semaphore_signal(barrier, inc=1, device_id=where_is(plane_, member_), device_id_type=MESH)

        for k in range(1, classes):
            for i in range(chips):
                greet(peer_plane(k), 2 * i + 1)
        greet(mate, chip * 2 + 1)
        for k in range(1, chips):
            greet(plane, lax.rem(chip + k, chips) * 2)
        pl.when(is_second)(lambda: greet(plane, chip * 2))

        fetch = pltpu.make_async_copy(kv_any, local, in_sems.at[1])
        fetch.start()
        q_fetch = pltpu.make_async_copy(q_any, q_ref, in_sems.at[0])
        q_fetch.start()
        doc_fetch = pltpu.make_async_copy(doc_any, doc_ref, in_sems.at[2])
        doc_fetch.start()

        for i, (h, e) in enumerate(maybe):
            @pl.when(block_of(e, 2 * kind + h) < first_live)
            def _():
                kvbuf[:, spare + i] = jnp.zeros((2, BLOCK, HEAD_WIDTH), kvbuf.dtype)

        @pl.when(is_first)
        def _():
            pl.semaphore_wait(barrier, members - 1)
            pl.semaphore_signal(plane_sem, inc=1, device_id=partner, device_id_type=MESH)

        @pl.when(is_second)
        def _():
            pl.semaphore_wait(plane_sem, 1)

        def remote(src, dst, sent, got, device):
            return pltpu.make_async_remote_copy(
                src_ref=src, dst_ref=dst, send_sem=sent, recv_sem=got, device_id=device, device_id_type=MESH)

        is_sure = sum((member == e).astype(jnp.int32) for e in sure)
        my_slot = sum(i * (member == e).astype(jnp.int32) for i, e in enumerate(sure))
        my_slot = my_slot + sum((spare + i) * ((member == e) & (half == h)).astype(jnp.int32)
                                for i, (h, e) in enumerate(maybe))
        my_slot_there = my_slot + len(sure) * is_sure

        def kv_part(c):
            first = pl.multiple_of(2 * c * heads // (QUERY_HEADS // KEY_VALUE_HEADS) * HEAD_WIDTH, HEAD_WIDTH)
            return local.at[:, :, pl.ds(first, HEAD_WIDTH)]

        def kv_copy(k):
            other = crossed(chip, k)
            return remote(kv_part(other), kvbuf.at[:, my_slot], kv_send.at[k], kv_recv.at[my_slot],
                          where_is(plane, other * 2 + 1))

        to_partner = remote(kv_part(chip), kvbuf.at[:, my_slot], kv_send.at[0], kv_recv.at[my_slot], partner)
        to_mate = remote(kv_part(chip), kvbuf.at[:, my_slot_there], kv_send.at[chips], kv_recv.at[my_slot_there],
                         mate_core)
        i_am_live = my_block >= first_live

        fetch.wait()

        @pl.when(i_am_live)
        def _():
            for k in steps:
                kv_copy(k).start()
            pltpu.make_async_copy(kv_part(chip), kvbuf.at[:, my_slot], kv_recv.at[my_slot]).start()
            to_partner.start()

        q_fetch.wait()
        for e in range(members):
            for h in range(heads):
                first = (e * heads + h) * HEAD_WIDTH
                wide[e, h * local_rows:(h + 1) * local_rows] = q_ref[:, first:first + HEAD_WIDTH].astype(jnp.float32)
            qsend[e] = wide[e].astype(qsend.dtype)
        doc_fetch.wait()

        def q_copy(k, j):
            e = lax.rem(member + j, members)
            return remote(qsend.at[e], qbuf.at[me], q_send, q_recv.at[kind], where_is(peer_plane(k), e))

        pltpu.make_async_copy(qsend.at[member], qbuf.at[me], q_recv.at[kind]).start()
        for j in range(1, members):
            q_copy(0, j).start()

        @pl.when(is_second)
        def _():
            pl.semaphore_wait(barrier, (classes - 1) * members + 2)
            pl.semaphore_signal(cross_sem, inc=1, device_id=partner, device_id_type=MESH)

        @pl.when(is_first)
        def _():
            pl.semaphore_wait(cross_sem, 1)

        pl.when(i_am_live)(to_mate.start)
        for k in range(1, classes):
            for j in range(members):
                q_copy(k, j).start()

        def landed(i):
            pltpu.make_async_copy(kvbuf.at[:, i], kvbuf.at[:, i], kv_recv.at[i]).wait()

        def to_first(i):
            return remote(kvbuf.at[:, i], kvbuf.at[:, i], pass_send.at[i], kv_recv.at[i], partner)

        def to_next(i, there):
            return remote(kvbuf.at[:, i], kvbuf.at[:, there], relay_send.at[i], kv_recv.at[there], mate_core)

        def in_order(of_half, first, step):
            for i, (h, e) in enumerate(maybe):
                is_live = (of_half == h) & (block_of(e, 2 * kind + h) >= first_live)
                pl.when(is_live)(lambda: step(spare + i, spare + i, e))
            for k in [0] + steps:
                for c in (1, 0):
                    e = crossed(chip, k) * 2 + c
                    i = sum(n * (e == f).astype(jnp.int32) for n, f in enumerate(sure))
                    found = sum((e == f).astype(jnp.int32) for f in sure) == 1
                    pl.when(found)(lambda: step(first + i, len(sure) + i, e))

        def own_slots(step):
            in_order(half, 0, step)

        def mate_slots(step):
            in_order(1 - half, len(sure), step)

        def hand_on(i, there, e):
            landed(i)

            @pl.when(is_second & (chip != e // 2))
            def _():
                to_next(i, there).start()
                to_first(i).start()

        def hand_over(i, there, e):
            landed(i)
            pl.when(is_second)(to_first(i).start)

        own_slots(hand_on)

        lane = lax.broadcasted_iota(jnp.int32, (chunk_rows, BLOCK), 1)
        row_index = lax.broadcasted_iota(jnp.int32, (chunk_rows, BLOCK), 0)
        row_query = row_index // slice_rows * local_rows + row_index % local_rows
        offset = (lax.broadcasted_iota(jnp.int32, (slice_rows, BLOCK), 1)
                  - lax.broadcasted_iota(jnp.int32, (slice_rows, BLOCK), 0))
        top_place, total_place = offset == 0, offset == slice_rows

        def part_of(source, members_part, first_slot, blocks):
            first, count = source // 2 * members + members_part.start, members_part.stop - members_part.start
            rows = slice(members_part.start * slice_rows, members_part.stop * slice_rows)
            q = qbuf[pl.ds(first, count)].reshape(count * slice_rows, HEAD_WIDTH)
            query_first = source * chunk_queries
            query_block = (query_first // BLOCK + 1) * stripe_blocks - 1
            in_block = row_query[rows] + query_first % BLOCK
            query_doc = doc_ref[query_block]
            held = slice(first_slot, first_slot + len(blocks))
            keys = kvbuf[0, held].reshape(len(blocks) * BLOCK, HEAD_WIDTH)
            values = kvbuf[1, held].reshape(len(blocks) * BLOCK, HEAD_WIDTH)
            scores = dot(q, keys, ((1,), (1,)))
            masked = []
            for i, b in enumerate(blocks):
                same = doc_ref[b] == query_doc
                whole = jnp.where(same & (b < query_block), BLOCK, -1)
                causal = jnp.where(same & (b == query_block), 0, -2 * BLOCK)
                limit = jnp.maximum(in_block + causal, whole)
                masked.append(jnp.where(lane[rows] <= limit, scores[:, i * BLOCK:(i + 1) * BLOCK], masked_score))
            top = masked[0]
            for s in masked[1:]:
                top = jnp.maximum(top, s)
            top = jnp.maximum(jnp.max(top, axis=1, keepdims=True), 0.5 * masked_score)
            weights = [jnp.exp2((s - top) * scale) for s in masked]
            total = weights[0]
            for p in weights[1:]:
                total = total + p
            total = jnp.sum(total, axis=1, keepdims=True)
            acc = dot(jnp.concatenate([p.astype(jnp.bfloat16) for p in weights], axis=1), values, ((1,), (0,)))
            return top, total, acc

        own_blocks = [block_of(e, plane) for e in sure]
        late_blocks = [block_of(e, mate) for e in sure] + [block_of(e, 2 * kind + h) for h, e in maybe]
        everyone = slice(0, members)
        pieces = [slice(0, members // 2), slice(members // 2, members)]

        def begin(source):
            mine = qbuf.at[pl.ds(source // 2 * members, members)]
            pltpu.make_async_copy(mine, mine, q_recv.at[source // 2]).wait()
            top, total, acc = part_of(source, everyone, 0, own_blocks)
            early_acc[source // 2] = acc
            early_top[source // 2] = jnp.broadcast_to(top, (chunk_rows, HEAD_WIDTH))
            early_total[source // 2] = jnp.broadcast_to(total, (chunk_rows, HEAD_WIDTH))

        def joined(parts):
            overall = parts[0][0]
            for part in parts[1:]:
                overall = jnp.maximum(overall, part[0])
            factors = [jnp.exp2((part[0] - overall) * scale) for part in parts]
            total = sum(f * part[1] for f, part in zip(factors, parts))
            acc = sum(f * part[2] for f, part in zip(factors, parts))
            return overall, total, acc

        def finish(source, members_part):
            rows = slice(members_part.start * slice_rows, members_part.stop * slice_rows)
            first, count = source // 2 * members + members_part.start, members_part.stop - members_part.start
            early = [ref[source // 2, rows] for ref in (early_top, early_total, early_acc)]
            top, total, acc = joined([early, part_of(source, members_part, len(sure), late_blocks)])
            osend[pl.ds(first, count)] = acc.astype(jnp.bfloat16).reshape(count, slice_rows, HEAD_WIDTH)
            for j in range(count):
                part = slice(j * slice_rows, (j + 1) * slice_rows)
                stats = jnp.where(top_place, top[part], jnp.where(total_place, total[part], 0.0))
                ssend[first + j] = jnp.sum(stats, axis=0, keepdims=True)

        def give(source, j):
            k = source // 2 * members + j
            device = where_is(source, j)
            return [remote(osend.at[k], obuf.at[kind, member], o_send, o_recv.at[kind], device),
                    remote(ssend.at[k], sbuf.at[kind, member], s_send, s_recv.at[kind], device)]

        begin(plane)
        for k in range(1, classes):
            begin(peer_plane(k))

        mate_slots(hand_over)

        for k in range(1, classes):
            for piece in pieces:
                finish(peer_plane(k), piece)
                for j in range(piece.start, piece.stop):
                    for copy in give(peer_plane(k), j):
                        copy.start()

        finish(plane, everyone)
        pltpu.make_async_copy(osend.at[me], obuf.at[kind, member], o_recv.at[kind]).start()
        pltpu.make_async_copy(ssend.at[me], sbuf.at[kind, member], s_recv.at[kind]).start()
        for i in range(1, members):
            for copy in give(plane, lax.rem(member + i, members)):
                copy.start()

        for g in range(classes):
            pltpu.make_async_copy(sbuf.at[g], sbuf.at[g], s_recv.at[g]).wait()
            pltpu.make_async_copy(obuf.at[g], obuf.at[g], o_recv.at[g]).wait()

        for e in range(members):
            column = lambda g, place: jnp.sum(jnp.where(place, sbuf[g, e], 0.0), axis=1, keepdims=True)
            tops = [column(g, top_place) for g in range(classes)]
            overall = tops[0]
            for t in tops[1:]:
                overall = jnp.maximum(overall, t)
            merged = weight = None
            for g in range(classes):
                factor = jnp.exp2((tops[g] - overall) * scale)
                term = factor * obuf[g, e].astype(jnp.float32)
                part = factor * column(g, total_place)
                merged = term if merged is None else merged + term
                weight = part if weight is None else weight + part
            wide[e] = merged / weight
            for h in range(heads):
                first = (e * heads + h) * HEAD_WIDTH
                out_ref[:, first:first + HEAD_WIDTH] = wide[e, h * local_rows:(h + 1) * local_rows].astype(out_ref.dtype)

        @pl.when(i_am_live)
        def _():
            to_partner.wait_send()
            for k in range(1, chips):
                kv_copy(k).wait_send()
            to_mate.wait_send()

        def own_sent(i, there, e):
            @pl.when(is_second & (chip != e // 2))
            def _():
                to_next(i, there).wait_send()
                to_first(i).wait_send()

        own_slots(own_sent)
        mate_slots(lambda i, there, e: pl.when(is_second)(to_first(i).wait_send))
        for buffer, sem in ((qbuf, q_send), (osend, o_send), (ssend, s_send)):
            others = buffer.at[pl.ds(0, messages - 1)]
            pltpu.make_async_copy(others, others, sem).wait()

    bf16, dma = jnp.bfloat16, pltpu.SemaphoreType.DMA
    signal = pltpu.SemaphoreType.REGULAR
    scratch = [
        pltpu.SMEM((blocks_n,), jnp.int32),
        pltpu.VMEM((local_rows, QUERY_HEADS * HEAD_WIDTH), bf16),
        pltpu.VMEM((2, BLOCK, KEY_VALUE_HEADS * HEAD_WIDTH), bf16),
        dma((3,)), signal, signal,
        pltpu.VMEM((members, slice_rows, HEAD_WIDTH), bf16),
        pltpu.VMEM((members, slice_rows, HEAD_WIDTH), jnp.float32),
        pltpu.VMEM((messages, slice_rows, HEAD_WIDTH), bf16),
        pltpu.VMEM((2, slots_n, BLOCK, HEAD_WIDTH), bf16),
        pltpu.VMEM((classes, chunk_rows, HEAD_WIDTH), jnp.float32),
        pltpu.VMEM((classes, chunk_rows, HEAD_WIDTH), jnp.float32),
        pltpu.VMEM((classes, chunk_rows, HEAD_WIDTH), jnp.float32),
        pltpu.VMEM((messages, slice_rows, HEAD_WIDTH), bf16),
        pltpu.VMEM((messages, 1, BLOCK), jnp.float32),
        pltpu.VMEM((classes, members, slice_rows, HEAD_WIDTH), bf16),
        pltpu.VMEM((classes, members, 1, BLOCK), jnp.float32),
        dma, dma((classes,)), dma((chips + 1,)), dma((slots_n,)), dma((slots_n,)), dma((slots_n,)),
        dma, dma((classes,)), dma, dma((classes,)),
    ]
    return kernel, scratch


def solution(mesh):
    rows_n, cols_n = mesh.shape["qrow"], mesh.shape["kcol"]

    def per_device(queries, keys_values, doc_blocks):
        local_rows = queries.shape[0]
        kernel, scratch = make_kernel(rows_n, cols_n, queries.shape[0], doc_blocks.shape[0])
        merged = pl.pallas_call(
            kernel,
            out_shape=pltpu.VMEM(queries.shape, queries.dtype),
            in_specs=[
                pl.BlockSpec(memory_space=pl.ANY),
                pl.BlockSpec(memory_space=pl.ANY),
                pl.BlockSpec(memory_space=pl.ANY),
            ],
            out_specs=pl.BlockSpec(memory_space=pltpu.VMEM),
            scratch_shapes=scratch,
            compiler_params=pltpu.CompilerParams(collective_id=0, has_side_effects=True),
        )(doc_blocks, queries, keys_values)

        return merged

    return jax.shard_map(
        per_device,
        mesh=mesh,
        in_specs=(P(("qrow", "kcol"), None), P(None, ("kcol", "qrow"), None), P()),
        out_specs=P(("qrow", "kcol"), None),
        check_vma=False,
    )
```

```python
import math

import jax
import jax.numpy as jnp
from jax import lax
from jax.experimental import pallas as pl
from jax.experimental.pallas import tpu as pltpu
from jax.sharding import PartitionSpec as P

QUERY_HEADS = 64
KEY_VALUE_HEADS = 4
HEAD_WIDTH = 128
BLOCK = 128
MESH = pl.DeviceIdType.MESH

masked_score = -1e30


def dot(a, b, dims):
    return lax.dot_general(a, b, (dims, ((), ())), preferred_element_type=jnp.float32)


def make_kernel(rows_n, cols_n, local_rows, blocks_n):
    fold = max(1, 8 // cols_n)
    planes = rows_n // fold
    members = fold * cols_n
    chips = members // 2
    classes = planes // 2
    heads = QUERY_HEADS // members
    slice_rows = local_rows * heads
    chunk_rows = members * slice_rows
    devices = rows_n * cols_n
    total_queries = devices * local_rows
    query_blocks = total_queries // BLOCK
    stripe_blocks = blocks_n // query_blocks
    chunk_queries = members * local_rows
    messages = classes * members
    assert BLOCK % chunk_queries == 0 and blocks_n == devices and cols_n % 2 == 0 and 2 * slice_rows <= BLOCK
    assert planes % 2 == 0
    first_live = max(0, stripe_blocks - 1 - blocks_n // 2)
    block_of = lambda e, p: (e % cols_n) * rows_n + p * fold + e // cols_n
    alive = lambda e, half: [block_of(e, p) >= first_live for p in range(half, planes, 2)]
    sure = [e for e in range(members) if all(alive(e, 0) + alive(e, 1))]
    maybe = [(half, e) for half in range(2) for e in range(members) if e not in sure and any(alive(e, half))]
    spare = 2 * len(sure)
    slots_n = spare + len(maybe)
    scale = math.log2(math.e) / math.sqrt(HEAD_WIDTH)

    assert sure and chips & (chips - 1) == 0
    steps = sorted(range(1, chips), key=lambda k: (bin(k).count("1"), -k))

    def crossed(chip, k):
        bits = [1 << n for n in range(chips.bit_length() - 1) if k >> n & 1]
        return chip + sum(bit * (1 - 2 * (chip // bit % 2)) for bit in bits)

    def where_is(plane, member):
        return (plane * fold + member // cols_n, member % cols_n)

    def kernel(doc_any, q_any, kv_any, out_ref, doc_ref, q_ref, local, in_sems, plane_sem, cross_sem,
               qsend, wide, qbuf, kvbuf, early_top, early_total, early_acc, osend, ssend, obuf, sbuf,
               q_send, q_recv, kv_send, kv_recv, pass_send, relay_send, o_send, o_recv, s_send, s_recv):
        row, col = lax.axis_index("qrow"), lax.axis_index("kcol")
        plane, core = row // fold, lax.rem(col, 2)
        member = (row % fold) * cols_n + col
        chip = member // 2
        half, kind = lax.rem(plane, 2), plane // 2
        mate = plane + 1 - 2 * half
        me = kind * members + member
        my_block = block_of(member, plane)
        partner = (row, col + 1 - 2 * core)
        mate_core = where_is(mate, chip * 2 + 1)
        is_first, is_second = core == 0, core == 1
        barrier = pltpu.get_barrier_semaphore()

        def peer_plane(k):
            return lax.rem(kind + k, classes) * 2 + half

        def greet(plane_, member_):
            pl.semaphore_signal(barrier, inc=1, device_id=where_is(plane_, member_), device_id_type=MESH)

        for k in range(1, chips):
            greet(plane, lax.rem(chip + k, chips) * 2 + 1)
        pl.when(is_first)(lambda: greet(plane, chip * 2 + 1))
        for k in range(1, classes):
            for i in range(chips):
                greet(peer_plane(k), 2 * i)
        greet(mate, chip * 2)

        fetch = pltpu.make_async_copy(kv_any, local, in_sems.at[1])
        fetch.start()
        q_fetch = pltpu.make_async_copy(q_any, q_ref, in_sems.at[0])
        q_fetch.start()
        doc_fetch = pltpu.make_async_copy(doc_any, doc_ref, in_sems.at[2])
        doc_fetch.start()

        for i, (h, e) in enumerate(maybe):
            @pl.when(block_of(e, 2 * kind + h) < first_live)
            def _():
                kvbuf[:, spare + i] = jnp.zeros((2, BLOCK, HEAD_WIDTH), kvbuf.dtype)

        @pl.when(is_second)
        def _():
            pl.semaphore_wait(barrier, members - 1)
            pl.semaphore_signal(plane_sem, inc=1, device_id=partner, device_id_type=MESH)

        @pl.when(is_first)
        def _():
            pl.semaphore_wait(plane_sem, 1)

        def remote(src, dst, sent, got, device):
            return pltpu.make_async_remote_copy(
                src_ref=src, dst_ref=dst, send_sem=sent, recv_sem=got, device_id=device, device_id_type=MESH)

        is_sure = sum((member == e).astype(jnp.int32) for e in sure)
        my_slot = sum(i * (member == e).astype(jnp.int32) for i, e in enumerate(sure))
        my_slot = my_slot + sum((spare + i) * ((member == e) & (half == h)).astype(jnp.int32)
                                for i, (h, e) in enumerate(maybe))
        my_slot_there = my_slot + len(sure) * is_sure

        def kv_part(c):
            first = pl.multiple_of(2 * c * heads // (QUERY_HEADS // KEY_VALUE_HEADS) * HEAD_WIDTH, HEAD_WIDTH)
            return local.at[:, :, pl.ds(first, HEAD_WIDTH)]

        def kv_copy(k):
            other = crossed(chip, k)
            return remote(kv_part(other), kvbuf.at[:, my_slot], kv_send.at[k], kv_recv.at[my_slot],
                          where_is(plane, other * 2 + 1))

        to_partner = remote(kv_part(chip), kvbuf.at[:, my_slot], kv_send.at[0], kv_recv.at[my_slot], partner)
        to_mate = remote(kv_part(chip), kvbuf.at[:, my_slot_there], kv_send.at[chips], kv_recv.at[my_slot_there],
                         mate_core)
        i_am_live = my_block >= first_live

        fetch.wait()

        @pl.when(i_am_live)
        def _():
            for k in steps:
                kv_copy(k).start()
            pltpu.make_async_copy(kv_part(chip), kvbuf.at[:, my_slot], kv_recv.at[my_slot]).start()
            to_partner.start()

        q_fetch.wait()
        for e in range(members):
            for h in range(heads):
                first = (e * heads + h) * HEAD_WIDTH
                wide[e, h * local_rows:(h + 1) * local_rows] = q_ref[:, first:first + HEAD_WIDTH].astype(jnp.float32)
            qsend[e] = wide[e].astype(qsend.dtype)
        doc_fetch.wait()

        def q_copy(k, j):
            e = lax.rem(member + j, members)
            return remote(qsend.at[e], qbuf.at[me], q_send, q_recv.at[kind], where_is(peer_plane(k), e))

        pltpu.make_async_copy(qsend.at[member], qbuf.at[me], q_recv.at[kind]).start()
        for j in range(1, members):
            q_copy(0, j).start()

        @pl.when(is_first)
        def _():
            pl.semaphore_wait(barrier, (classes - 1) * members + 2)
            pl.semaphore_signal(cross_sem, inc=1, device_id=partner, device_id_type=MESH)

        @pl.when(is_second)
        def _():
            pl.semaphore_wait(cross_sem, 1)

        pl.when(i_am_live)(to_mate.start)
        for k in range(1, classes):
            for j in range(members):
                q_copy(k, j).start()

        def landed(i):
            pltpu.make_async_copy(kvbuf.at[:, i], kvbuf.at[:, i], kv_recv.at[i]).wait()

        def to_first(i):
            return remote(kvbuf.at[:, i], kvbuf.at[:, i], pass_send.at[i], kv_recv.at[i], partner)

        def to_next(i, there):
            return remote(kvbuf.at[:, i], kvbuf.at[:, there], relay_send.at[i], kv_recv.at[there], mate_core)

        def in_order(of_half, first, step):
            for k in [0] + steps:
                for c in (1, 0):
                    e = crossed(chip, k) * 2 + c
                    i = sum(n * (e == f).astype(jnp.int32) for n, f in enumerate(sure))
                    found = sum((e == f).astype(jnp.int32) for f in sure) == 1
                    pl.when(found)(lambda: step(first + i, len(sure) + i, e))
                    for n, (h, f) in enumerate(maybe):
                        if f % 2 == c:
                            is_live = (e == f) & (of_half == h) & (block_of(f, 2 * kind + h) >= first_live)
                            pl.when(is_live)(lambda: step(spare + n, spare + n, f))

        def own_slots(step):
            in_order(half, 0, step)

        def mate_slots(step):
            in_order(1 - half, len(sure), step)

        def hand_on(i, there, e):
            landed(i)

            @pl.when(is_second & (chip != e // 2))
            def _():
                to_next(i, there).start()
                to_first(i).start()

        def hand_over(i, there, e):
            landed(i)
            pl.when(is_second)(to_first(i).start)

        own_slots(hand_on)

        lane = lax.broadcasted_iota(jnp.int32, (chunk_rows, BLOCK), 1)
        row_index = lax.broadcasted_iota(jnp.int32, (chunk_rows, BLOCK), 0)
        row_query = row_index // slice_rows * local_rows + row_index % local_rows
        offset = (lax.broadcasted_iota(jnp.int32, (slice_rows, BLOCK), 1)
                  - lax.broadcasted_iota(jnp.int32, (slice_rows, BLOCK), 0))
        top_place, total_place = offset == 0, offset == slice_rows

        def part_of(source, members_part, first_slot, blocks):
            first, count = source // 2 * members + members_part.start, members_part.stop - members_part.start
            rows = slice(members_part.start * slice_rows, members_part.stop * slice_rows)
            q = qbuf[pl.ds(first, count)].reshape(count * slice_rows, HEAD_WIDTH)
            query_first = source * chunk_queries
            query_block = (query_first // BLOCK + 1) * stripe_blocks - 1
            in_block = row_query[rows] + query_first % BLOCK
            query_doc = doc_ref[query_block]
            held = slice(first_slot, first_slot + len(blocks))
            keys = kvbuf[0, held].reshape(len(blocks) * BLOCK, HEAD_WIDTH)
            values = kvbuf[1, held].reshape(len(blocks) * BLOCK, HEAD_WIDTH)
            scores = dot(q, keys, ((1,), (1,)))
            masked = []
            for i, b in enumerate(blocks):
                same = doc_ref[b] == query_doc
                whole = jnp.where(same & (b < query_block), BLOCK, -1)
                causal = jnp.where(same & (b == query_block), 0, -2 * BLOCK)
                limit = jnp.maximum(in_block + causal, whole)
                masked.append(jnp.where(lane[rows] <= limit, scores[:, i * BLOCK:(i + 1) * BLOCK], masked_score))
            top = masked[0]
            for s in masked[1:]:
                top = jnp.maximum(top, s)
            top = jnp.maximum(jnp.max(top, axis=1, keepdims=True), 0.5 * masked_score)
            weights = [jnp.exp2((s - top) * scale) for s in masked]
            total = weights[0]
            for p in weights[1:]:
                total = total + p
            total = jnp.sum(total, axis=1, keepdims=True)
            acc = dot(jnp.concatenate([p.astype(jnp.bfloat16) for p in weights], axis=1), values, ((1,), (0,)))
            return top, total, acc

        own_blocks = [block_of(e, plane) for e in sure]
        late_blocks = [block_of(e, mate) for e in sure] + [block_of(e, 2 * kind + h) for h, e in maybe]
        everyone = slice(0, members)
        pieces = [slice(0, members // 2), slice(members // 2, members)]

        def begin(source):
            mine = qbuf.at[pl.ds(source // 2 * members, members)]
            pltpu.make_async_copy(mine, mine, q_recv.at[source // 2]).wait()
            top, total, acc = part_of(source, everyone, 0, own_blocks)
            early_acc[source // 2] = acc
            early_top[source // 2] = jnp.broadcast_to(top, (chunk_rows, HEAD_WIDTH))
            early_total[source // 2] = jnp.broadcast_to(total, (chunk_rows, HEAD_WIDTH))

        def joined(parts):
            overall = parts[0][0]
            for part in parts[1:]:
                overall = jnp.maximum(overall, part[0])
            factors = [jnp.exp2((part[0] - overall) * scale) for part in parts]
            total = sum(f * part[1] for f, part in zip(factors, parts))
            acc = sum(f * part[2] for f, part in zip(factors, parts))
            return overall, total, acc

        def finish(source, members_part):
            rows = slice(members_part.start * slice_rows, members_part.stop * slice_rows)
            first, count = source // 2 * members + members_part.start, members_part.stop - members_part.start
            early = [ref[source // 2, rows] for ref in (early_top, early_total, early_acc)]
            top, total, acc = joined([early, part_of(source, members_part, len(sure), late_blocks)])
            osend[pl.ds(first, count)] = acc.astype(jnp.bfloat16).reshape(count, slice_rows, HEAD_WIDTH)
            for j in range(count):
                part = slice(j * slice_rows, (j + 1) * slice_rows)
                stats = jnp.where(top_place, top[part], jnp.where(total_place, total[part], 0.0))
                ssend[first + j] = jnp.sum(stats, axis=0, keepdims=True)

        def give(source, j):
            k = source // 2 * members + j
            device = where_is(source, j)
            return [remote(osend.at[k], obuf.at[kind, member], o_send, o_recv.at[kind], device),
                    remote(ssend.at[k], sbuf.at[kind, member], s_send, s_recv.at[kind], device)]

        begin(plane)
        for k in range(1, classes):
            begin(peer_plane(k))

        mate_slots(hand_over)

        for k in range(1, classes):
            for piece in pieces:
                finish(peer_plane(k), piece)
                for j in range(piece.start, piece.stop):
                    for copy in give(peer_plane(k), j):
                        copy.start()

        finish(plane, everyone)
        pltpu.make_async_copy(osend.at[me], obuf.at[kind, member], o_recv.at[kind]).start()
        pltpu.make_async_copy(ssend.at[me], sbuf.at[kind, member], s_recv.at[kind]).start()
        for i in range(1, members):
            for copy in give(plane, lax.rem(member + i, members)):
                copy.start()

        for g in range(classes):
            pltpu.make_async_copy(sbuf.at[g], sbuf.at[g], s_recv.at[g]).wait()
            pltpu.make_async_copy(obuf.at[g], obuf.at[g], o_recv.at[g]).wait()

        for e in range(members):
            column = lambda g, place: jnp.sum(jnp.where(place, sbuf[g, e], 0.0), axis=1, keepdims=True)
            tops = [column(g, top_place) for g in range(classes)]
            overall = tops[0]
            for t in tops[1:]:
                overall = jnp.maximum(overall, t)
            merged = weight = None
            for g in range(classes):
                factor = jnp.exp2((tops[g] - overall) * scale)
                term = factor * obuf[g, e].astype(jnp.float32)
                part = factor * column(g, total_place)
                merged = term if merged is None else merged + term
                weight = part if weight is None else weight + part
            wide[e] = merged / weight
            for h in range(heads):
                first = (e * heads + h) * HEAD_WIDTH
                out_ref[:, first:first + HEAD_WIDTH] = wide[e, h * local_rows:(h + 1) * local_rows].astype(out_ref.dtype)

        @pl.when(i_am_live)
        def _():
            to_partner.wait_send()
            for k in range(1, chips):
                kv_copy(k).wait_send()
            to_mate.wait_send()

        def own_sent(i, there, e):
            @pl.when(is_second & (chip != e // 2))
            def _():
                to_next(i, there).wait_send()
                to_first(i).wait_send()

        own_slots(own_sent)
        mate_slots(lambda i, there, e: pl.when(is_second)(to_first(i).wait_send))
        for buffer, sem in ((qbuf, q_send), (osend, o_send), (ssend, s_send)):
            others = buffer.at[pl.ds(0, messages - 1)]
            pltpu.make_async_copy(others, others, sem).wait()

    bf16, dma = jnp.bfloat16, pltpu.SemaphoreType.DMA
    signal = pltpu.SemaphoreType.REGULAR
    scratch = [
        pltpu.SMEM((blocks_n,), jnp.int32),
        pltpu.VMEM((local_rows, QUERY_HEADS * HEAD_WIDTH), bf16),
        pltpu.VMEM((2, BLOCK, KEY_VALUE_HEADS * HEAD_WIDTH), bf16),
        dma((3,)), signal, signal,
        pltpu.VMEM((members, slice_rows, HEAD_WIDTH), bf16),
        pltpu.VMEM((members, slice_rows, HEAD_WIDTH), jnp.float32),
        pltpu.VMEM((messages, slice_rows, HEAD_WIDTH), bf16),
        pltpu.VMEM((2, slots_n, BLOCK, HEAD_WIDTH), bf16),
        pltpu.VMEM((classes, chunk_rows, HEAD_WIDTH), jnp.float32),
        pltpu.VMEM((classes, chunk_rows, HEAD_WIDTH), jnp.float32),
        pltpu.VMEM((classes, chunk_rows, HEAD_WIDTH), jnp.float32),
        pltpu.VMEM((messages, slice_rows, HEAD_WIDTH), bf16),
        pltpu.VMEM((messages, 1, BLOCK), jnp.float32),
        pltpu.VMEM((classes, members, slice_rows, HEAD_WIDTH), bf16),
        pltpu.VMEM((classes, members, 1, BLOCK), jnp.float32),
        dma, dma((classes,)), dma((chips + 1,)), dma((slots_n,)), dma((slots_n,)), dma((slots_n,)),
        dma, dma((classes,)), dma, dma((classes,)),
    ]
    return kernel, scratch


def solution(mesh):
    rows_n, cols_n = mesh.shape["qrow"], mesh.shape["kcol"]

    def per_device(queries, keys_values, doc_blocks):
        local_rows = queries.shape[0]
        kernel, scratch = make_kernel(rows_n, cols_n, queries.shape[0], doc_blocks.shape[0])
        merged = pl.pallas_call(
            kernel,
            out_shape=pltpu.VMEM(queries.shape, queries.dtype),
            in_specs=[
                pl.BlockSpec(memory_space=pl.ANY),
                pl.BlockSpec(memory_space=pl.ANY),
                pl.BlockSpec(memory_space=pl.ANY),
            ],
            out_specs=pl.BlockSpec(memory_space=pltpu.VMEM),
            scratch_shapes=scratch,
            compiler_params=pltpu.CompilerParams(collective_id=0, has_side_effects=True),
        )(doc_blocks, queries, keys_values)

        return merged

    return jax.shard_map(
        per_device,
        mesh=mesh,
        in_specs=(P(("qrow", "kcol"), None), P(None, ("kcol", "qrow"), None), P()),
        out_specs=P(("qrow", "kcol"), None),
        check_vma=False,
    )
```

```python
import math

import jax
import jax.numpy as jnp
from jax import lax
from jax.experimental import pallas as pl
from jax.experimental.pallas import tpu as pltpu
from jax.sharding import PartitionSpec as P

QUERY_HEADS = 64
KEY_VALUE_HEADS = 4
HEAD_WIDTH = 128
BLOCK = 128
MESH = pl.DeviceIdType.MESH

masked_score = -1e30


def dot(a, b, dims):
    return lax.dot_general(a, b, (dims, ((), ())), preferred_element_type=jnp.float32)


def make_kernel(rows_n, cols_n, local_rows, blocks_n):
    fold = max(1, 8 // cols_n)
    planes = rows_n // fold
    members = fold * cols_n
    chips = members // 2
    classes = planes // 2
    heads = QUERY_HEADS // members
    slice_rows = local_rows * heads
    chunk_rows = members * slice_rows
    devices = rows_n * cols_n
    total_queries = devices * local_rows
    query_blocks = total_queries // BLOCK
    stripe_blocks = blocks_n // query_blocks
    chunk_queries = members * local_rows
    messages = classes * members
    assert BLOCK % chunk_queries == 0 and blocks_n == devices and cols_n % 2 == 0 and 2 * slice_rows <= BLOCK
    assert planes % 2 == 0
    first_live = max(0, stripe_blocks - 1 - blocks_n // 2)
    block_of = lambda e, p: (e % cols_n) * rows_n + p * fold + e // cols_n
    alive = lambda e, half: [block_of(e, p) >= first_live for p in range(half, planes, 2)]
    sure = [e for e in range(members) if all(alive(e, 0) + alive(e, 1))]
    maybe = [(half, e) for half in range(2) for e in range(members) if e not in sure and any(alive(e, half))]
    spare = 2 * len(sure)
    slots_n = spare + len(maybe)
    scale = math.log2(math.e) / math.sqrt(HEAD_WIDTH)

    assert chips + 1 <= slots_n
    assert sure and chips & (chips - 1) == 0
    steps = sorted(range(1, chips), key=lambda k: (bin(k).count("1"), -k))

    def crossed(chip, k):
        bits = [1 << n for n in range(chips.bit_length() - 1) if k >> n & 1]
        return chip + sum(bit * (1 - 2 * (chip // bit % 2)) for bit in bits)

    def where_is(plane, member):
        return (plane * fold + member // cols_n, member % cols_n)

    def kernel(doc_any, q_any, kv_any, out_ref, doc_ref, q_ref, local, plane_sem, cross_sem,
               qsend, wide, qbuf, kvbuf, early_top, early_total, early_acc, late_top, late_total, late_weights, osend, ssend, obuf, sbuf,
               q_send, q_recv, kv_send, kv_recv, pass_send, o_send, o_recv, s_send, s_recv):
        row, col = lax.axis_index("qrow"), lax.axis_index("kcol")
        plane, core = row // fold, lax.rem(col, 2)
        member = (row % fold) * cols_n + col
        chip = member // 2
        half, kind = lax.rem(plane, 2), plane // 2
        mate = plane + 1 - 2 * half
        me = kind * members + member
        my_block = block_of(member, plane)
        partner = (row, col + 1 - 2 * core)
        mate_core = where_is(mate, chip * 2 + 1)
        is_first, is_second = core == 0, core == 1
        barrier = pltpu.get_barrier_semaphore()
        fetch = pltpu.make_async_copy(kv_any, local, kv_send)
        fetch.start()

        def peer_plane(k):
            return lax.rem(kind + k, classes) * 2 + half

        def greet(plane_, member_):
            pl.semaphore_signal(barrier, inc=1, device_id=where_is(plane_, member_), device_id_type=MESH)

        for k in range(1, chips):
            greet(plane, lax.rem(chip + k, chips) * 2 + 1)
        pl.when(is_first)(lambda: greet(plane, chip * 2 + 1))
        for k in range(1, classes):
            for i in range(chips):
                greet(peer_plane(k), 2 * i)
        greet(mate, chip * 2)

        q_fetch = pltpu.make_async_copy(q_any, q_ref, q_send)
        q_fetch.start()
        doc_fetch = pltpu.make_async_copy(doc_any, doc_ref, o_send)
        doc_fetch.start()

        for i, (h, e) in enumerate(maybe):
            @pl.when(block_of(e, 2 * kind + h) < first_live)
            def _():
                kvbuf[:, spare + i] = jnp.zeros((2, BLOCK, HEAD_WIDTH), kvbuf.dtype)

        @pl.when(is_second)
        def _():
            pl.semaphore_wait(barrier, members - 1)
            pl.semaphore_signal(plane_sem, inc=1, device_id=partner, device_id_type=MESH)

        @pl.when(is_first)
        def _():
            pl.semaphore_wait(plane_sem, 1)

        def remote(src, dst, sent, got, device):
            return pltpu.make_async_remote_copy(
                src_ref=src, dst_ref=dst, send_sem=sent, recv_sem=got, device_id=device, device_id_type=MESH)

        is_sure = sum((member == e).astype(jnp.int32) for e in sure)
        my_slot = sum(i * (member == e).astype(jnp.int32) for i, e in enumerate(sure))
        my_slot = my_slot + sum((spare + i) * ((member == e) & (half == h)).astype(jnp.int32)
                                for i, (h, e) in enumerate(maybe))
        my_slot_there = my_slot + len(sure) * is_sure

        def kv_part(t, c):
            first = pl.multiple_of(2 * c * heads // (QUERY_HEADS // KEY_VALUE_HEADS) * HEAD_WIDTH, HEAD_WIDTH)
            return local.at[t, :, pl.ds(first, HEAD_WIDTH)]

        def kv_copy(t, k):
            other = crossed(chip, k)
            return remote(kv_part(t, other), kvbuf.at[t, my_slot], kv_send, kv_recv.at[t, my_slot],
                          where_is(plane, other * 2 + 1))

        def to_partner(t):
            return remote(kv_part(t, chip), kvbuf.at[t, my_slot], kv_send, kv_recv.at[t, my_slot], partner)

        def to_mate(t):
            return remote(kv_part(t, chip), kvbuf.at[t, my_slot_there], kv_send,
                          kv_recv.at[t, my_slot_there], mate_core)

        i_am_live = my_block >= first_live

        fetch.wait()

        @pl.when(i_am_live)
        def _():
            for t in range(2):
                for k in steps:
                    kv_copy(t, k).start()
            for t in range(2):
                pltpu.make_async_copy(kv_part(t, chip), kvbuf.at[t, my_slot], kv_recv.at[t, my_slot]).start()
                to_partner(t).start()

        q_fetch.wait()
        for e in range(members):
            for h in range(heads):
                first = (e * heads + h) * HEAD_WIDTH
                wide[e, h * local_rows:(h + 1) * local_rows] = q_ref[:, first:first + HEAD_WIDTH].astype(jnp.float32)
            qsend[e] = wide[e].astype(qsend.dtype)
        doc_fetch.wait()

        def q_copy(k, e):
            return remote(qsend.at[e], qbuf.at[me], q_send, q_recv.at[kind], where_is(peer_plane(k), e))

        def q_to(k, chips_crossed):
            for n in chips_crossed:
                for c in range(2):
                    if n == 0 and k == 0:
                        if c == 0:
                            q_copy(0, member + 1 - 2 * core).start()
                    else:
                        q_copy(k, crossed(chip, n) * 2 + c).start()

        near = [n for n in range(chips) if n % 2 == 0]
        far = [n for n in range(chips) if n % 2 == 1]

        def q_far():
            for k in range(classes):
                q_to(k, far)

        pltpu.make_async_copy(qsend.at[member], qbuf.at[me], q_recv.at[kind]).start()
        q_to(0, near)

        @pl.when(is_first)
        def _():
            pl.semaphore_wait(barrier, (classes - 1) * members + 2)
            pl.semaphore_signal(cross_sem, inc=1, device_id=partner, device_id_type=MESH)

        @pl.when(is_second)
        def _():
            pl.semaphore_wait(cross_sem, 1)

        @pl.when(i_am_live)
        def _():
            to_mate(0).start()
            to_mate(1).start()

        for k in range(1, classes):
            q_to(k, near)
        q_far()

        def landed(t, i):
            pltpu.make_async_copy(kvbuf.at[t, i], kvbuf.at[t, i], kv_recv.at[t, i]).wait()

        def to_first(t, i):
            return remote(kvbuf.at[t, i], kvbuf.at[t, i], pass_send.at[i], kv_recv.at[t, i], partner)

        def to_next(t, i, there):
            return remote(kvbuf.at[t, i], kvbuf.at[t, there], pass_send.at[i], kv_recv.at[t, there], mate_core)

        def in_order(of_half, first, step):
            for k in [0] + steps:
                for c in (1, 0):
                    e = crossed(chip, k) * 2 + c
                    i = sum(n * (e == f).astype(jnp.int32) for n, f in enumerate(sure))
                    found = sum((e == f).astype(jnp.int32) for f in sure) == 1
                    pl.when(found)(lambda: step(first + i, len(sure) + i, e))
                    for n, (h, f) in enumerate(maybe):
                        if f % 2 == c:
                            is_live = (e == f) & (of_half == h) & (block_of(f, 2 * kind + h) >= first_live)
                            pl.when(is_live)(lambda: step(spare + n, spare + n, f))

        def own_slots(step):
            in_order(half, 0, step)

        def mate_slots(step):
            in_order(1 - half, len(sure), step)

        def hand_on(t):
            def step(i, there, e):
                landed(t, i)

                @pl.when(is_second & (chip != e // 2))
                def _():
                    to_next(t, i, there).start()
                    to_first(t, i).start()
            return step

        def hand_over(t):
            def step(i, there, e):
                landed(t, i)
                to_first(t, i).start()
            return step

        own_slots(hand_on(0))
        own_slots(hand_on(1))

        lane = lax.broadcasted_iota(jnp.int32, (chunk_rows, BLOCK), 1)
        row_index = lax.broadcasted_iota(jnp.int32, (chunk_rows, BLOCK), 0)
        row_query = row_index // slice_rows * local_rows + row_index % local_rows
        offset = (lax.broadcasted_iota(jnp.int32, (slice_rows, BLOCK), 1)
                  - lax.broadcasted_iota(jnp.int32, (slice_rows, BLOCK), 0))
        top_place, total_place = offset == 0, offset == slice_rows

        def weigh(k, members_part, first_slot, blocks):
            first, count = k * members + members_part.start, members_part.stop - members_part.start
            rows = slice(members_part.start * slice_rows, members_part.stop * slice_rows)
            q = qbuf[pl.ds(first, count)].reshape(count * slice_rows, HEAD_WIDTH)
            query_first = (2 * k + half) * chunk_queries
            query_block = (query_first // BLOCK + 1) * stripe_blocks - 1
            in_block = row_query[rows] + query_first % BLOCK
            query_doc = doc_ref[query_block]
            held = slice(first_slot, first_slot + len(blocks))
            keys = kvbuf[0, held].reshape(len(blocks) * BLOCK, HEAD_WIDTH)
            scores = dot(q, keys, ((1,), (1,)))
            masked = []
            for i, b in enumerate(blocks):
                same = doc_ref[b] == query_doc
                whole = jnp.where(same & (b < query_block), BLOCK, -1)
                causal = jnp.where(same & (b == query_block), 0, -2 * BLOCK)
                limit = jnp.maximum(in_block + causal, whole)
                masked.append(jnp.where(lane[rows] <= limit, scores[:, i * BLOCK:(i + 1) * BLOCK], masked_score))
            top = masked[0]
            for s in masked[1:]:
                top = jnp.maximum(top, s)
            top = jnp.maximum(jnp.max(top, axis=1, keepdims=True), 0.5 * masked_score)
            weights = [jnp.exp2((s - top) * scale) for s in masked]
            total = weights[0]
            for p in weights[1:]:
                total = total + p
            total = jnp.sum(total, axis=1, keepdims=True)
            return top, total, jnp.concatenate([p.astype(jnp.bfloat16) for p in weights], axis=1)

        def summed(weights, first_slot):
            count = weights.shape[1] // BLOCK
            values = kvbuf[1, first_slot:first_slot + count].reshape(count * BLOCK, HEAD_WIDTH)
            return dot(weights, values, ((1,), (0,)))

        def part_of(k, members_part, first_slot, blocks):
            top, total, weights = weigh(k, members_part, first_slot, blocks)
            return top, total, summed(weights, first_slot)

        own_blocks = [block_of(e, plane) for e in sure]
        late_blocks = [block_of(e, mate) for e in sure] + [block_of(e, 2 * kind + h) for h, e in maybe]
        everyone = slice(0, members)
        pieces = [slice(0, members // 2), slice(members // 2, members)]

        def await_queries(k):
            mine = qbuf.at[pl.ds(k * members, members)]
            pltpu.make_async_copy(mine, mine, q_recv.at[k]).wait()

        def begin(k):
            await_queries(k)
            top, total, acc = part_of(k, everyone, 0, own_blocks)
            early_acc[...] = acc
            early_top[...] = jnp.broadcast_to(top, (chunk_rows, HEAD_WIDTH))
            early_total[...] = jnp.broadcast_to(total, (chunk_rows, HEAD_WIDTH))

        def joined(parts):
            overall = parts[0][0]
            for part in parts[1:]:
                overall = jnp.maximum(overall, part[0])
            factors = [jnp.exp2((part[0] - overall) * scale) for part in parts]
            total = sum(f * part[1] for f, part in zip(factors, parts))
            acc = sum(f * part[2] for f, part in zip(factors, parts))
            return overall, total, acc

        def put(k, members_part, top, total, acc):
            first, count = k * members + members_part.start, members_part.stop - members_part.start
            osend[pl.ds(first, count)] = acc.astype(jnp.bfloat16).reshape(count, slice_rows, HEAD_WIDTH)
            for j in range(count):
                part = slice(j * slice_rows, (j + 1) * slice_rows)
                stats = jnp.where(top_place, top[part], jnp.where(total_place, total[part], 0.0))
                ssend[first + j] = jnp.sum(stats, axis=0, keepdims=True)

        def rows_of(members_part):
            return slice(members_part.start * slice_rows, members_part.stop * slice_rows)

        def prepare(k, members_part):
            rows = rows_of(members_part)
            top, total, weights = weigh(k, members_part, len(sure), late_blocks)
            late_top[rows] = jnp.broadcast_to(top, (weights.shape[0], HEAD_WIDTH))
            late_total[rows] = jnp.broadcast_to(total, (weights.shape[0], HEAD_WIDTH))
            late_weights[rows] = weights

        def finish(k, members_part):
            rows = rows_of(members_part)
            early = [ref[rows] for ref in (early_top, early_total, early_acc)]
            late = [late_top[rows], late_total[rows], summed(late_weights[rows], len(sure))]
            put(k, members_part, *joined([early, late]))

        def give(k, members_part):
            for j in range(members_part.start, members_part.stop):
                n = k * members + j
                device = where_is(2 * k + half, j)
                to_me = (kind == k) & (member == j)

                @pl.when(to_me)
                def _():
                    pltpu.make_async_copy(osend.at[n], obuf.at[kind, member], o_recv).start()
                    pltpu.make_async_copy(ssend.at[n], sbuf.at[kind, member], s_recv).start()

                @pl.when(jnp.logical_not(to_me))
                def _():
                    remote(osend.at[n], obuf.at[kind, member], o_send, o_recv, device).start()
                    remote(ssend.at[n], sbuf.at[kind, member], s_send, s_recv, device).start()

        begin(0)

        @pl.when(is_second)
        def _():
            mate_slots(hand_over(0))
            mate_slots(hand_over(1))

        pl.when(is_first)(lambda: mate_slots(lambda i, there, e: landed(0, i)))

        prepare(0, everyone)

        pl.when(is_first)(lambda: mate_slots(lambda i, there, e: landed(1, i)))

        for piece in pieces:
            finish(0, piece)
            give(0, piece)

        def attend(k):
            await_queries(k)
            put(k, everyone, *part_of(k, everyone, 0, own_blocks + late_blocks))
            give(k, everyone)

        if classes <= 4:
            for k in range(1, classes):
                attend(k)
        else:
            pl.loop(1, classes)(attend)

        @pl.when(i_am_live)
        def _():
            sent = kvbuf.at[:, pl.ds(0, chips + 1)]
            pltpu.make_async_copy(sent, sent, kv_send).wait()

        def handed_on(i, there, e):
            @pl.when(is_second & (chip != e // 2))
            def _():
                sent = kvbuf.at[:, pl.ds(0, 2)]
                pltpu.make_async_copy(sent, sent, pass_send.at[i]).wait()

        def handed_over(i, there, e):
            sent = kvbuf.at[:, i]
            pl.when(is_second)(pltpu.make_async_copy(sent, sent, pass_send.at[i]).wait)

        own_slots(handed_on)
        mate_slots(handed_over)
        for buffer, sem in ((qbuf, q_send), (osend, o_send), (ssend, s_send)):
            others = buffer.at[pl.ds(0, messages - 1)]
            pltpu.make_async_copy(others, others, sem).wait()

        pltpu.make_async_copy(sbuf, sbuf, s_recv).wait()
        pltpu.make_async_copy(obuf, obuf, o_recv).wait()

        for e in range(members):
            column = lambda g, place: jnp.sum(jnp.where(place, sbuf[g, e], 0.0), axis=1, keepdims=True)
            tops = [column(g, top_place) for g in range(classes)]
            overall = tops[0]
            for t in tops[1:]:
                overall = jnp.maximum(overall, t)
            merged = weight = None
            for g in range(classes):
                factor = jnp.exp2((tops[g] - overall) * scale)
                term = factor * obuf[g, e].astype(jnp.float32)
                part = factor * column(g, total_place)
                merged = term if merged is None else merged + term
                weight = part if weight is None else weight + part
            wide[e] = merged / weight
            for h in range(heads):
                first = (e * heads + h) * HEAD_WIDTH
                out_ref[:, first:first + HEAD_WIDTH] = wide[e, h * local_rows:(h + 1) * local_rows].astype(out_ref.dtype)

    bf16, dma = jnp.bfloat16, pltpu.SemaphoreType.DMA
    signal = pltpu.SemaphoreType.REGULAR
    scratch = [
        pltpu.SMEM((blocks_n,), jnp.int32),
        pltpu.VMEM((local_rows, QUERY_HEADS * HEAD_WIDTH), bf16),
        pltpu.VMEM((2, BLOCK, KEY_VALUE_HEADS * HEAD_WIDTH), bf16),
        signal, signal,
        pltpu.VMEM((members, slice_rows, HEAD_WIDTH), bf16),
        pltpu.VMEM((members, slice_rows, HEAD_WIDTH), jnp.float32),
        pltpu.VMEM((messages, slice_rows, HEAD_WIDTH), bf16),
        pltpu.VMEM((2, slots_n, BLOCK, HEAD_WIDTH), bf16),
        pltpu.VMEM((chunk_rows, HEAD_WIDTH), jnp.float32),
        pltpu.VMEM((chunk_rows, HEAD_WIDTH), jnp.float32),
        pltpu.VMEM((chunk_rows, HEAD_WIDTH), jnp.float32),
        pltpu.VMEM((chunk_rows, HEAD_WIDTH), jnp.float32),
        pltpu.VMEM((chunk_rows, HEAD_WIDTH), jnp.float32),
        pltpu.VMEM((chunk_rows, (slots_n - len(sure)) * BLOCK), bf16),
        pltpu.VMEM((messages, slice_rows, HEAD_WIDTH), bf16),
        pltpu.VMEM((messages, 1, BLOCK), jnp.float32),
        pltpu.VMEM((classes, members, slice_rows, HEAD_WIDTH), bf16),
        pltpu.VMEM((classes, members, 1, BLOCK), jnp.float32),
        dma, dma((classes,)), dma, dma((2, slots_n)), dma((slots_n,)),
        dma, dma, dma, dma,
    ]
    return kernel, scratch


def solution(mesh):
    rows_n, cols_n = mesh.shape["qrow"], mesh.shape["kcol"]

    def per_device(queries, keys_values, doc_blocks):
        local_rows = queries.shape[0]
        kernel, scratch = make_kernel(rows_n, cols_n, queries.shape[0], doc_blocks.shape[0])
        merged = pl.pallas_call(
            kernel,
            out_shape=pltpu.VMEM(queries.shape, queries.dtype),
            in_specs=[
                pl.BlockSpec(memory_space=pl.ANY),
                pl.BlockSpec(memory_space=pl.ANY),
                pl.BlockSpec(memory_space=pl.ANY),
            ],
            out_specs=pl.BlockSpec(memory_space=pltpu.VMEM),
            scratch_shapes=scratch,
            compiler_params=pltpu.CompilerParams(collective_id=0, has_side_effects=True),
        )(doc_blocks, queries, keys_values)

        return merged

    return jax.shard_map(
        per_device,
        mesh=mesh,
        in_specs=(P(("qrow", "kcol"), None), P(None, ("kcol", "qrow"), None), P()),
        out_specs=P(("qrow", "kcol"), None),
        check_vma=False,
    )
```

```python
import math

import jax
import jax.numpy as jnp
from jax import lax
from jax.experimental import pallas as pl
from jax.experimental.pallas import tpu as pltpu
from jax.sharding import PartitionSpec as P

QUERY_HEADS = 64
KEY_VALUE_HEADS = 4
HEAD_WIDTH = 128
BLOCK = 128
MESH = pl.DeviceIdType.MESH

masked_score = -1e30


def dot(a, b, dims):
    return lax.dot_general(a, b, (dims, ((), ())), preferred_element_type=jnp.float32)


def make_kernel(rows_n, cols_n, local_rows, blocks_n):
    fold = max(1, 8 // cols_n)
    planes = rows_n // fold
    members = fold * cols_n
    chips = members // 2
    classes = planes // 2
    heads = QUERY_HEADS // members
    slice_rows = local_rows * heads
    chunk_rows = members * slice_rows
    devices = rows_n * cols_n
    total_queries = devices * local_rows
    query_blocks = total_queries // BLOCK
    stripe_blocks = blocks_n // query_blocks
    chunk_queries = members * local_rows
    messages = classes * members
    assert BLOCK % chunk_queries == 0 and blocks_n == devices and cols_n % 2 == 0 and 2 * slice_rows <= BLOCK
    assert planes % 2 == 0
    first_live = max(0, stripe_blocks - 1 - blocks_n // 2)
    block_of = lambda e, p: (e % cols_n) * rows_n + p * fold + e // cols_n
    alive = lambda e, half: [block_of(e, p) >= first_live for p in range(half, planes, 2)]
    sure = [e for e in range(members) if all(alive(e, 0) + alive(e, 1))]
    maybe = [(half, e) for half in range(2) for e in range(members) if e not in sure and any(alive(e, half))]
    spare = 2 * len(sure)
    slots_n = spare + len(maybe)
    scale = math.log2(math.e) / math.sqrt(HEAD_WIDTH)

    assert chips + 1 <= slots_n
    assert sure and chips & (chips - 1) == 0
    steps = sorted(range(1, chips), key=lambda k: (bin(k).count("1"), -k))

    routes = [steps, steps[::-1]]

    def crossed(chip, k):
        bits = [1 << n for n in range(chips.bit_length() - 1) if k >> n & 1]
        return chip + sum(bit * (1 - 2 * (chip // bit % 2)) for bit in bits)

    def where_is(plane, member):
        return (plane * fold + member // cols_n, member % cols_n)

    def kernel(doc_any, q_any, kv_any, out_ref, doc_ref, q_ref, local, plane_sem, cross_sem,
               qsend, wide, qbuf, kvbuf, early_top, early_total, early_acc, late_top, late_total, late_weights, osend, ssend, obuf, sbuf,
               q_send, q_recv, kv_send, kv_recv, pass_send, o_send, o_recv, s_send, s_recv):
        row, col = lax.axis_index("qrow"), lax.axis_index("kcol")
        plane, core = row // fold, lax.rem(col, 2)
        member = (row % fold) * cols_n + col
        chip = member // 2
        half, kind = lax.rem(plane, 2), plane // 2
        mate = plane + 1 - 2 * half
        me = kind * members + member
        my_block = block_of(member, plane)
        partner = (row, col + 1 - 2 * core)
        mate_core = where_is(mate, chip * 2 + 1)
        is_first, is_second = core == 0, core == 1
        barrier = pltpu.get_barrier_semaphore()
        fetches = [pltpu.make_async_copy(kv_any.at[t], local.at[t], sem) for t, sem in enumerate((kv_send, s_send))]
        for fetch in fetches:
            fetch.start()

        def peer_plane(k):
            return lax.rem(kind + k, classes) * 2 + half

        def greet(plane_, member_):
            pl.semaphore_signal(barrier, inc=1, device_id=where_is(plane_, member_), device_id_type=MESH)

        for k in range(1, chips):
            greet(plane, lax.rem(chip + k, chips) * 2 + 1)
        pl.when(is_first)(lambda: greet(plane, chip * 2 + 1))
        for k in range(1, classes):
            for i in range(chips):
                greet(peer_plane(k), 2 * i)
        greet(mate, chip * 2)

        q_fetch = pltpu.make_async_copy(q_any, q_ref, q_send)
        q_fetch.start()
        doc_fetch = pltpu.make_async_copy(doc_any, doc_ref, o_send)
        doc_fetch.start()

        for i, (h, e) in enumerate(maybe):
            @pl.when(block_of(e, 2 * kind + h) < first_live)
            def _():
                kvbuf[:, spare + i] = jnp.zeros((2, BLOCK, HEAD_WIDTH), kvbuf.dtype)

        @pl.when(is_second)
        def _():
            pl.semaphore_wait(barrier, members - 1)
            pl.semaphore_signal(plane_sem, inc=1, device_id=partner, device_id_type=MESH)

        @pl.when(is_first)
        def _():
            pl.semaphore_wait(plane_sem, 1)

        def remote(src, dst, sent, got, device):
            return pltpu.make_async_remote_copy(
                src_ref=src, dst_ref=dst, send_sem=sent, recv_sem=got, device_id=device, device_id_type=MESH)

        is_sure = sum((member == e).astype(jnp.int32) for e in sure)
        my_slot = sum(i * (member == e).astype(jnp.int32) for i, e in enumerate(sure))
        my_slot = my_slot + sum((spare + i) * ((member == e) & (half == h)).astype(jnp.int32)
                                for i, (h, e) in enumerate(maybe))
        my_slot_there = my_slot + len(sure) * is_sure

        def kv_part(t, c):
            first = pl.multiple_of(2 * c * heads // (QUERY_HEADS // KEY_VALUE_HEADS) * HEAD_WIDTH, HEAD_WIDTH)
            return local.at[t, :, pl.ds(first, HEAD_WIDTH)]

        def kv_copy(t, k):
            other = crossed(chip, k)
            return remote(kv_part(t, other), kvbuf.at[t, my_slot], kv_send, kv_recv.at[t, my_slot],
                          where_is(plane, other * 2 + 1))

        def to_partner(t):
            return remote(kv_part(t, chip), kvbuf.at[t, my_slot], kv_send, kv_recv.at[t, my_slot], partner)

        def to_mate(t):
            return remote(kv_part(t, chip), kvbuf.at[t, my_slot_there], kv_send,
                          kv_recv.at[t, my_slot_there], mate_core)

        i_am_live = my_block >= first_live

        fetches[0].wait()

        @pl.when(i_am_live)
        def _():
            for k in routes[0]:
                kv_copy(0, k).start()

        fetches[1].wait()

        @pl.when(i_am_live)
        def _():
            for k in routes[1]:
                kv_copy(1, k).start()
            for t in range(2):
                pltpu.make_async_copy(kv_part(t, chip), kvbuf.at[t, my_slot], kv_recv.at[t, my_slot]).start()
                to_partner(t).start()

        q_fetch.wait()
        for e in range(members):
            for h in range(heads):
                first = (e * heads + h) * HEAD_WIDTH
                wide[e, h * local_rows:(h + 1) * local_rows] = q_ref[:, first:first + HEAD_WIDTH].astype(jnp.float32)
            qsend[e] = wide[e].astype(qsend.dtype)
        doc_fetch.wait()

        def q_copy(k, e):
            return remote(qsend.at[e], qbuf.at[me], q_send, q_recv.at[kind], where_is(peer_plane(k), e))

        def q_to(k, chips_crossed):
            for n in chips_crossed:
                for c in range(2):
                    if n == 0 and k == 0:
                        if c == 0:
                            q_copy(0, member + 1 - 2 * core).start()
                    else:
                        q_copy(k, crossed(chip, n) * 2 + c).start()

        near = [n for n in range(chips) if n % 2 == 0]
        far = [n for n in range(chips) if n % 2 == 1]

        keys_first = (is_sure == 1) & (kind > 0)

        def q_far():
            for k in [*range(1, classes), 0]:
                q_to(k, far)

        pltpu.make_async_copy(qsend.at[member], qbuf.at[me], q_recv.at[kind]).start()
        q_to(0, near)

        @pl.when(is_first)
        def _():
            pl.semaphore_wait(barrier, (classes - 1) * members + 2)
            pl.semaphore_signal(cross_sem, inc=1, device_id=partner, device_id_type=MESH)

        @pl.when(is_second)
        def _():
            pl.semaphore_wait(cross_sem, 1)

        @pl.when(i_am_live)
        def _():
            to_mate(0).start()
            to_mate(1).start()

        for k in range(1, classes):
            q_to(k, near)
        pl.when(jnp.logical_not(keys_first))(q_far)

        def landed(t, i):
            pltpu.make_async_copy(kvbuf.at[t, i], kvbuf.at[t, i], kv_recv.at[t, i]).wait()

        def to_first(t, i):
            return remote(kvbuf.at[t, i], kvbuf.at[t, i], pass_send.at[i], kv_recv.at[t, i], partner)

        def to_next(t, i, there):
            return remote(kvbuf.at[t, i], kvbuf.at[t, there], pass_send.at[i], kv_recv.at[t, there], mate_core)

        def in_order(of_half, first, step, t=0):
            def unsure(k):
                for n, (h, f) in enumerate(maybe):
                    is_live = (crossed(chip, k) == f // 2) & (of_half == h) & (block_of(f, 2 * kind + h) >= first_live)
                    pl.when(is_live)(lambda: step(spare + n, spare + n, f))

            if t == 1:
                for k in [0] + steps:
                    unsure(k)
            for k in [0] + routes[t]:
                for c in (1, 0):
                    e = crossed(chip, k) * 2 + c
                    i = sum(n * (e == f).astype(jnp.int32) for n, f in enumerate(sure))
                    found = sum((e == f).astype(jnp.int32) for f in sure) == 1
                    pl.when(found)(lambda: step(first + i, len(sure) + i, e))
                if t == 0:
                    unsure(k)

        def own_slots(step, t=0):
            in_order(half, 0, step, t)

        def mate_slots(step, t=0):
            in_order(1 - half, len(sure), step, t)

        def hand_on(t):
            def step(i, there, e):
                landed(t, i)

                @pl.when(is_second & (chip != e // 2))
                def _():
                    to_next(t, i, there).start()
                    to_first(t, i).start()
            return step

        def hand_over(t):
            def step(i, there, e):
                landed(t, i)
                to_first(t, i).start()
            return step

        own_slots(hand_on(0))
        pl.when(keys_first)(q_far)
        own_slots(hand_on(1), 1)

        lane = lax.broadcasted_iota(jnp.int32, (chunk_rows, BLOCK), 1)
        row_index = lax.broadcasted_iota(jnp.int32, (chunk_rows, BLOCK), 0)
        row_query = row_index // slice_rows * local_rows + row_index % local_rows
        place = (lax.broadcasted_iota(jnp.int32, (slice_rows, BLOCK), 1)
                 == lax.broadcasted_iota(jnp.int32, (slice_rows, BLOCK), 0))
        as_row = lambda column: jnp.sum(jnp.where(place, column, 0.0), axis=0, keepdims=True)
        as_column = lambda row: jnp.sum(jnp.where(place, row, 0.0), axis=1, keepdims=True)

        def weigh(k, members_part, first_slot, blocks):
            first, count = k * members + members_part.start, members_part.stop - members_part.start
            rows = slice(members_part.start * slice_rows, members_part.stop * slice_rows)
            q = qbuf[pl.ds(first, count)].reshape(count * slice_rows, HEAD_WIDTH)
            query_first = (2 * k + half) * chunk_queries
            query_block = (query_first // BLOCK + 1) * stripe_blocks - 1
            in_block = row_query[rows] + query_first % BLOCK
            query_doc = doc_ref[query_block]
            held = slice(first_slot, first_slot + len(blocks))
            keys = kvbuf[0, held].reshape(len(blocks) * BLOCK, HEAD_WIDTH)
            scores = dot(q, keys, ((1,), (1,)))
            masked = []
            for i, b in enumerate(blocks):
                same = doc_ref[b] == query_doc
                whole = jnp.where(same & (b < query_block), BLOCK, -1)
                causal = jnp.where(same & (b == query_block), 0, -2 * BLOCK)
                limit = jnp.maximum(in_block + causal, whole)
                masked.append(jnp.where(lane[rows] <= limit, scores[:, i * BLOCK:(i + 1) * BLOCK], masked_score))
            top = masked[0]
            for s in masked[1:]:
                top = jnp.maximum(top, s)
            top = jnp.maximum(jnp.max(top, axis=1, keepdims=True), 0.5 * masked_score)
            weights = [jnp.exp2((s - top) * scale) for s in masked]
            total = weights[0]
            for p in weights[1:]:
                total = total + p
            total = jnp.sum(total, axis=1, keepdims=True)
            return top, total, jnp.concatenate([p.astype(jnp.bfloat16) for p in weights], axis=1)

        def summed(weights, first_slot):
            count = weights.shape[1] // BLOCK
            values = kvbuf[1, first_slot:first_slot + count].reshape(count * BLOCK, HEAD_WIDTH)
            return dot(weights, values, ((1,), (0,)))

        def part_of(k, members_part, first_slot, blocks):
            top, total, weights = weigh(k, members_part, first_slot, blocks)
            return top, total, summed(weights, first_slot)

        own_blocks = [block_of(e, plane) for e in sure]
        late_blocks = [block_of(e, mate) for e in sure] + [block_of(e, 2 * kind + h) for h, e in maybe]
        everyone = slice(0, members)
        pieces = [slice(0, members // 2), slice(members // 2, members)]

        def await_queries(k):
            mine = qbuf.at[pl.ds(k * members, members)]
            pltpu.make_async_copy(mine, mine, q_recv.at[k]).wait()

        def begin(k):
            await_queries(k)
            top, total, acc = part_of(k, everyone, 0, own_blocks)
            early_acc[...] = acc
            early_top[...] = jnp.broadcast_to(top, (chunk_rows, HEAD_WIDTH))
            early_total[...] = jnp.broadcast_to(total, (chunk_rows, HEAD_WIDTH))

        def joined(parts):
            overall = parts[0][0]
            for part in parts[1:]:
                overall = jnp.maximum(overall, part[0])
            factors = [jnp.exp2((part[0] - overall) * scale) for part in parts]
            total = sum(f * part[1] for f, part in zip(factors, parts))
            acc = sum(f * part[2] for f, part in zip(factors, parts))
            return overall, total, acc

        def put(k, members_part, top, total, acc):
            first, count = k * members + members_part.start, members_part.stop - members_part.start
            osend[pl.ds(first, count)] = acc.astype(jnp.bfloat16).reshape(count, slice_rows, HEAD_WIDTH)
            for j in range(count):
                part = slice(j * slice_rows, (j + 1) * slice_rows)
                ssend[first + j] = jnp.concatenate([as_row(top[part]), as_row(total[part])], axis=0)

        def rows_of(members_part):
            return slice(members_part.start * slice_rows, members_part.stop * slice_rows)

        def prepare(k, members_part):
            rows = rows_of(members_part)
            top, total, weights = weigh(k, members_part, len(sure), late_blocks)
            late_top[rows] = jnp.broadcast_to(top, (weights.shape[0], HEAD_WIDTH))
            late_total[rows] = jnp.broadcast_to(total, (weights.shape[0], HEAD_WIDTH))
            late_weights[rows] = weights

        def finish(k, members_part):
            rows = rows_of(members_part)
            early = [ref[rows] for ref in (early_top, early_total, early_acc)]
            late = [late_top[rows], late_total[rows], summed(late_weights[rows], len(sure))]
            put(k, members_part, *joined([early, late]))

        def give(k, members_part):
            for j in range(members_part.start, members_part.stop):
                n = k * members + j
                device = where_is(2 * k + half, j)
                to_me = (kind == k) & (member == j)

                @pl.when(to_me)
                def _():
                    pltpu.make_async_copy(osend.at[n], obuf.at[kind, member], o_recv).start()
                    pltpu.make_async_copy(ssend.at[n], sbuf.at[kind, member], s_recv).start()

                @pl.when(jnp.logical_not(to_me))
                def _():
                    remote(ssend.at[n], sbuf.at[kind, member], s_send, s_recv, device).start()
                    remote(osend.at[n], obuf.at[kind, member], o_send, o_recv, device).start()

        begin(0)

        def wait_only(t):
            return lambda i, there, e: landed(t, i)

        pl.when(is_second)(lambda: mate_slots(hand_over(0)))
        pl.when(is_first)(lambda: mate_slots(wait_only(0)))

        prepare(0, everyone)

        pl.when(is_second)(lambda: mate_slots(hand_over(1), 1))
        pl.when(is_first)(lambda: mate_slots(wait_only(1), 1))

        for piece in pieces:
            finish(0, piece)
            give(0, piece)

        def attend(k):
            await_queries(k)
            put(k, everyone, *part_of(k, everyone, 0, own_blocks + late_blocks))
            give(k, everyone)

        if classes <= 4:
            for k in range(1, classes):
                attend(k)
        else:
            pl.loop(1, classes)(attend)

        @pl.when(i_am_live)
        def _():
            sent = kvbuf.at[:, pl.ds(0, chips + 1)]
            pltpu.make_async_copy(sent, sent, kv_send).wait()

        def handed_on(i, there, e):
            @pl.when(is_second & (chip != e // 2))
            def _():
                sent = kvbuf.at[:, pl.ds(0, 2)]
                pltpu.make_async_copy(sent, sent, pass_send.at[i]).wait()

        def handed_over(i, there, e):
            sent = kvbuf.at[:, i]
            pl.when(is_second)(pltpu.make_async_copy(sent, sent, pass_send.at[i]).wait)

        own_slots(handed_on)
        mate_slots(handed_over)
        for buffer, sem in ((qbuf, q_send), (osend, o_send), (ssend, s_send)):
            others = buffer.at[pl.ds(0, messages - 1)]
            pltpu.make_async_copy(others, others, sem).wait()

        pltpu.make_async_copy(sbuf, sbuf, s_recv).wait()
        shares = []
        for e in range(members):
            tops = [sbuf[g, e, 0:1] for g in range(classes)]
            overall = tops[0]
            for t in tops[1:]:
                overall = jnp.maximum(overall, t)
            factors = [jnp.exp2((t - overall) * scale) for t in tops]
            weight = sum(f * sbuf[g, e, 1:2] for g, f in enumerate(factors))
            weight = jnp.where(weight > 0.0, weight, 1.0)
            shares.append([as_column(f / weight) for f in factors])

        pltpu.make_async_copy(obuf, obuf, o_recv).wait()

        for e in range(members):
            wide[e] = sum(share * obuf[g, e].astype(jnp.float32) for g, share in enumerate(shares[e]))
            for h in range(heads):
                first = (e * heads + h) * HEAD_WIDTH
                out_ref[:, first:first + HEAD_WIDTH] = wide[e, h * local_rows:(h + 1) * local_rows].astype(out_ref.dtype)

    bf16, dma = jnp.bfloat16, pltpu.SemaphoreType.DMA
    signal = pltpu.SemaphoreType.REGULAR
    scratch = [
        pltpu.SMEM((blocks_n,), jnp.int32),
        pltpu.VMEM((local_rows, QUERY_HEADS * HEAD_WIDTH), bf16),
        pltpu.VMEM((2, BLOCK, KEY_VALUE_HEADS * HEAD_WIDTH), bf16),
        signal, signal,
        pltpu.VMEM((members, slice_rows, HEAD_WIDTH), bf16),
        pltpu.VMEM((members, slice_rows, HEAD_WIDTH), jnp.float32),
        pltpu.VMEM((messages, slice_rows, HEAD_WIDTH), bf16),
        pltpu.VMEM((2, slots_n, BLOCK, HEAD_WIDTH), bf16),
        pltpu.VMEM((chunk_rows, HEAD_WIDTH), jnp.float32),
        pltpu.VMEM((chunk_rows, HEAD_WIDTH), jnp.float32),
        pltpu.VMEM((chunk_rows, HEAD_WIDTH), jnp.float32),
        pltpu.VMEM((chunk_rows, HEAD_WIDTH), jnp.float32),
        pltpu.VMEM((chunk_rows, HEAD_WIDTH), jnp.float32),
        pltpu.VMEM((chunk_rows, (slots_n - len(sure)) * BLOCK), bf16),
        pltpu.VMEM((messages, slice_rows, HEAD_WIDTH), bf16),
        pltpu.VMEM((messages, 2, BLOCK), jnp.float32),
        pltpu.VMEM((classes, members, slice_rows, HEAD_WIDTH), bf16),
        pltpu.VMEM((classes, members, 2, BLOCK), jnp.float32),
        dma, dma((classes,)), dma, dma((2, slots_n)), dma((slots_n,)),
        dma, dma, dma, dma,
    ]
    return kernel, scratch


def solution(mesh):
    rows_n, cols_n = mesh.shape["qrow"], mesh.shape["kcol"]

    def per_device(queries, keys_values, doc_blocks):
        local_rows = queries.shape[0]
        kernel, scratch = make_kernel(rows_n, cols_n, queries.shape[0], doc_blocks.shape[0])
        merged = pl.pallas_call(
            kernel,
            out_shape=pltpu.VMEM(queries.shape, queries.dtype),
            in_specs=[
                pl.BlockSpec(memory_space=pl.ANY),
                pl.BlockSpec(memory_space=pl.ANY),
                pl.BlockSpec(memory_space=pl.ANY),
            ],
            out_specs=pl.BlockSpec(memory_space=pltpu.VMEM),
            scratch_shapes=scratch,
            compiler_params=pltpu.CompilerParams(collective_id=0, has_side_effects=True),
        )(doc_blocks, queries, keys_values)

        return merged

    return jax.shard_map(
        per_device,
        mesh=mesh,
        in_specs=(P(("qrow", "kcol"), None), P(None, ("kcol", "qrow"), None), P()),
        out_specs=P(("qrow", "kcol"), None),
        check_vma=False,
    )
```

```python
import math

import jax
import jax.numpy as jnp
from jax import lax
from jax.experimental import pallas as pl
from jax.experimental.pallas import tpu as pltpu
from jax.sharding import PartitionSpec as P

QUERY_HEADS = 64
KEY_VALUE_HEADS = 4
HEAD_WIDTH = 128
BLOCK = 128
MESH = pl.DeviceIdType.MESH

masked_score = -1e30


def dot(a, b, dims):
    return lax.dot_general(a, b, (dims, ((), ())), preferred_element_type=jnp.float32)


def make_kernel(rows_n, cols_n, local_rows, blocks_n):
    fold = max(1, 8 // cols_n)
    planes = rows_n // fold
    members = fold * cols_n
    chips = members // 2
    classes = planes // 2
    heads = QUERY_HEADS // members
    slice_rows = local_rows * heads
    chunk_rows = members * slice_rows
    devices = rows_n * cols_n
    total_queries = devices * local_rows
    query_blocks = total_queries // BLOCK
    stripe_blocks = blocks_n // query_blocks
    chunk_queries = members * local_rows
    messages = classes * members
    assert BLOCK % chunk_queries == 0 and blocks_n == devices and cols_n % 2 == 0 and 2 * slice_rows <= BLOCK
    assert planes % 2 == 0
    first_live = max(0, stripe_blocks - 1 - blocks_n // 2)
    block_of = lambda e, p: (e % cols_n) * rows_n + p * fold + e // cols_n
    alive = lambda e, half: [block_of(e, p) >= first_live for p in range(half, planes, 2)]
    sure = [e for e in range(members) if all(alive(e, 0) + alive(e, 1))]
    maybe = [(half, e) for half in range(2) for e in range(members) if e not in sure and any(alive(e, half))]
    spare = 2 * len(sure)
    slots_n = spare + len(maybe)
    scale = math.log2(math.e) / math.sqrt(HEAD_WIDTH)

    assert chips + 1 <= slots_n
    assert sure and chips & (chips - 1) == 0
    steps = sorted(range(1, chips), key=lambda k: (bin(k).count("1"), -k))

    routes = [steps, steps[::-1]]

    def crossed(chip, k):
        bits = [1 << n for n in range(chips.bit_length() - 1) if k >> n & 1]
        return chip + sum(bit * (1 - 2 * (chip // bit % 2)) for bit in bits)

    def where_is(plane, member):
        return (plane * fold + member // cols_n, member % cols_n)

    def kernel(doc_any, q_any, kv_any, out_ref, doc_ref, q_ref, local, plane_sem, cross_sem,
               qsend, wide, qbuf, kvbuf, early_top, early_total, early_acc, late_top, late_total, late_weights, osend, ssend, obuf, sbuf,
               q_send, q_recv, kv_send, kv_recv, pass_send, o_send, o_recv, s_send, s_recv):
        row, col = lax.axis_index("qrow"), lax.axis_index("kcol")
        plane, core = row // fold, lax.rem(col, 2)
        member = (row % fold) * cols_n + col
        chip = member // 2
        half, kind = lax.rem(plane, 2), plane // 2
        mate = plane + 1 - 2 * half
        me = kind * members + member
        my_block = block_of(member, plane)
        partner = (row, col + 1 - 2 * core)
        mate_core = where_is(mate, chip * 2 + 1)
        is_first, is_second = core == 0, core == 1
        barrier = pltpu.get_barrier_semaphore()
        fetches = [pltpu.make_async_copy(kv_any.at[t], local.at[t], sem) for t, sem in enumerate((kv_send, s_send))]
        for fetch in fetches:
            fetch.start()

        def peer_plane(k):
            return lax.rem(kind + k, classes) * 2 + half

        def greet(plane_, member_):
            pl.semaphore_signal(barrier, inc=1, device_id=where_is(plane_, member_), device_id_type=MESH)

        for k in range(1, chips):
            greet(plane, lax.rem(chip + k, chips) * 2 + 1)
        pl.when(is_first)(lambda: greet(plane, chip * 2 + 1))
        for k in range(1, classes):
            for i in range(chips):
                greet(peer_plane(k), 2 * i)
        greet(mate, chip * 2)

        q_fetch = pltpu.make_async_copy(q_any, q_ref, q_send)
        q_fetch.start()
        doc_fetch = pltpu.make_async_copy(doc_any, doc_ref, o_send)
        doc_fetch.start()

        for i, (h, e) in enumerate(maybe):
            @pl.when(block_of(e, 2 * kind + h) < first_live)
            def _():
                kvbuf[:, spare + i] = jnp.zeros((2, BLOCK, HEAD_WIDTH), kvbuf.dtype)

        @pl.when(is_second)
        def _():
            pl.semaphore_wait(barrier, members - 1)
            pl.semaphore_signal(plane_sem, inc=1, device_id=partner, device_id_type=MESH)

        @pl.when(is_first)
        def _():
            pl.semaphore_wait(plane_sem, 1)

        def remote(src, dst, sent, got, device):
            return pltpu.make_async_remote_copy(
                src_ref=src, dst_ref=dst, send_sem=sent, recv_sem=got, device_id=device, device_id_type=MESH)

        is_sure = sum((member == e).astype(jnp.int32) for e in sure)
        my_slot = sum(i * (member == e).astype(jnp.int32) for i, e in enumerate(sure))
        my_slot = my_slot + sum((spare + i) * ((member == e) & (half == h)).astype(jnp.int32)
                                for i, (h, e) in enumerate(maybe))
        my_slot_there = my_slot + len(sure) * is_sure

        def kv_part(t, c):
            first = pl.multiple_of(2 * c * heads // (QUERY_HEADS // KEY_VALUE_HEADS) * HEAD_WIDTH, HEAD_WIDTH)
            return local.at[t, :, pl.ds(first, HEAD_WIDTH)]

        def kv_copy(t, k):
            other = crossed(chip, k)
            return remote(kv_part(t, other), kvbuf.at[t, my_slot], kv_send, kv_recv.at[t, my_slot],
                          where_is(plane, other * 2 + 1))

        def to_partner(t):
            return remote(kv_part(t, chip), kvbuf.at[t, my_slot], kv_send, kv_recv.at[t, my_slot], partner)

        def to_mate(t):
            return remote(kv_part(t, chip), kvbuf.at[t, my_slot_there], kv_send,
                          kv_recv.at[t, my_slot_there], mate_core)

        i_am_live = my_block >= first_live

        fetches[0].wait()

        @pl.when(i_am_live)
        def _():
            for k in routes[0]:
                kv_copy(0, k).start()

        fetches[1].wait()

        @pl.when(i_am_live)
        def _():
            for k in routes[1]:
                kv_copy(1, k).start()
            for t in range(2):
                pltpu.make_async_copy(kv_part(t, chip), kvbuf.at[t, my_slot], kv_recv.at[t, my_slot]).start()
                to_partner(t).start()

        q_fetch.wait()
        for e in range(members):
            for h in range(heads):
                first = (e * heads + h) * HEAD_WIDTH
                wide[e, h * local_rows:(h + 1) * local_rows] = q_ref[:, first:first + HEAD_WIDTH].astype(jnp.float32)
            qsend[e] = wide[e].astype(qsend.dtype)
        doc_fetch.wait()

        def q_copy(k, e):
            return remote(qsend.at[e], qbuf.at[me], q_send, q_recv.at[kind], where_is(peer_plane(k), e))

        def q_to(k, chips_crossed):
            for n in chips_crossed:
                for c in range(2):
                    if n == 0 and k == 0:
                        if c == 0:
                            q_copy(0, member + 1 - 2 * core).start()
                    else:
                        q_copy(k, crossed(chip, n) * 2 + c).start()

        near = [n for n in range(chips) if n % 2 == 0]
        far = [n for n in range(chips) if n % 2 == 1]

        keys_first = (is_sure == 1) & (kind > 0)

        def q_far():
            for k in [*range(1, classes), 0]:
                q_to(k, far)

        pltpu.make_async_copy(qsend.at[member], qbuf.at[me], q_recv.at[kind]).start()
        q_to(0, near)

        @pl.when(is_first)
        def _():
            pl.semaphore_wait(barrier, (classes - 1) * members + 2)
            pl.semaphore_signal(cross_sem, inc=1, device_id=partner, device_id_type=MESH)

        @pl.when(is_second)
        def _():
            pl.semaphore_wait(cross_sem, 1)

        @pl.when(i_am_live)
        def _():
            to_mate(0).start()
            to_mate(1).start()

        for k in range(1, classes):
            q_to(k, near)
        pl.when(jnp.logical_not(keys_first))(q_far)

        def landed(t, i):
            pltpu.make_async_copy(kvbuf.at[t, i], kvbuf.at[t, i], kv_recv.at[t, i]).wait()

        def to_first(t, i):
            return remote(kvbuf.at[t, i], kvbuf.at[t, i], pass_send.at[i], kv_recv.at[t, i], partner)

        def to_next(t, i, there):
            return remote(kvbuf.at[t, i], kvbuf.at[t, there], pass_send.at[i], kv_recv.at[t, there], mate_core)

        def in_order(of_half, first, step, t=0):
            def unsure(k):
                for n, (h, f) in enumerate(maybe):
                    is_live = (crossed(chip, k) == f // 2) & (of_half == h) & (block_of(f, 2 * kind + h) >= first_live)
                    pl.when(is_live)(lambda: step(spare + n, spare + n, f))

            if t == 1:
                for k in [0] + steps:
                    unsure(k)
            for k in [0] + routes[t]:
                for c in (1, 0):
                    e = crossed(chip, k) * 2 + c
                    i = sum(n * (e == f).astype(jnp.int32) for n, f in enumerate(sure))
                    found = sum((e == f).astype(jnp.int32) for f in sure) == 1
                    pl.when(found)(lambda: step(first + i, len(sure) + i, e))
                if t == 0:
                    unsure(k)

        def own_slots(step, t=0):
            in_order(half, 0, step, t)

        def mate_slots(step, t=0):
            in_order(1 - half, len(sure), step, t)

        def hand_on(t):
            def step(i, there, e):
                landed(t, i)

                @pl.when(is_second & (chip != e // 2))
                def _():
                    to_next(t, i, there).start()
                    to_first(t, i).start()
            return step

        def hand_over(t):
            def step(i, there, e):
                landed(t, i)
                to_first(t, i).start()
            return step

        own_slots(hand_on(0))
        pl.when(keys_first)(q_far)
        own_slots(hand_on(1), 1)

        lane = lax.broadcasted_iota(jnp.int32, (chunk_rows, BLOCK), 1)
        row_index = lax.broadcasted_iota(jnp.int32, (chunk_rows, BLOCK), 0)
        key_ahead = lane - (row_index // slice_rows * local_rows + row_index % local_rows)
        place = (lax.broadcasted_iota(jnp.int32, (slice_rows, BLOCK), 1)
                 == lax.broadcasted_iota(jnp.int32, (slice_rows, BLOCK), 0))
        as_row = lambda column: jnp.sum(jnp.where(place, column, 0.0), axis=0, keepdims=True)
        as_column = lambda row: jnp.sum(jnp.where(place, row, 0.0), axis=1, keepdims=True)

        def weigh(k, members_part, first_slot, blocks):
            first, count = k * members + members_part.start, members_part.stop - members_part.start
            rows = slice(members_part.start * slice_rows, members_part.stop * slice_rows)
            q = qbuf[pl.ds(first, count)].reshape(count * slice_rows, HEAD_WIDTH)
            query_first = (2 * k + half) * chunk_queries
            query_block = (query_first // BLOCK + 1) * stripe_blocks - 1
            ahead = key_ahead[rows] - query_first % BLOCK
            query_doc = doc_ref[query_block]
            held = slice(first_slot, first_slot + len(blocks))
            keys = kvbuf[0, held].reshape(len(blocks) * BLOCK, HEAD_WIDTH)
            scores = dot(q, keys, ((1,), (1,)))
            masked = []
            for i, b in enumerate(blocks):
                same = doc_ref[b] == query_doc
                reach = jnp.where(b < query_block, BLOCK, jnp.where(b == query_block, 0, -2 * BLOCK))
                reach = jnp.where(same, reach, -2 * BLOCK)
                masked.append(jnp.where(ahead <= reach, scores[:, i * BLOCK:(i + 1) * BLOCK], masked_score))
            top = masked[0]
            for s in masked[1:]:
                top = jnp.maximum(top, s)
            top = jnp.maximum(jnp.max(top, axis=1, keepdims=True), 0.5 * masked_score)
            weights = [jnp.exp2((s - top) * scale) for s in masked]
            total = weights[0]
            for p in weights[1:]:
                total = total + p
            total = jnp.sum(total, axis=1, keepdims=True)
            return top, total, jnp.concatenate([p.astype(jnp.bfloat16) for p in weights], axis=1)

        def summed(weights, first_slot):
            count = weights.shape[1] // BLOCK
            values = kvbuf[1, first_slot:first_slot + count].reshape(count * BLOCK, HEAD_WIDTH)
            return dot(weights, values, ((1,), (0,)))

        def part_of(k, members_part, first_slot, blocks):
            top, total, weights = weigh(k, members_part, first_slot, blocks)
            return top, total, summed(weights, first_slot)

        own_blocks = [block_of(e, plane) for e in sure]
        late_blocks = [block_of(e, mate) for e in sure] + [block_of(e, 2 * kind + h) for h, e in maybe]
        everyone = slice(0, members)
        pieces = [slice(0, members // 2), slice(members // 2, members)]

        def await_queries(k):
            mine = qbuf.at[pl.ds(k * members, members)]
            pltpu.make_async_copy(mine, mine, q_recv.at[k]).wait()

        def begin(k):
            await_queries(k)
            top, total, acc = part_of(k, everyone, 0, own_blocks)
            early_acc[...] = acc
            early_top[...] = jnp.broadcast_to(top, (chunk_rows, HEAD_WIDTH))
            early_total[...] = jnp.broadcast_to(total, (chunk_rows, HEAD_WIDTH))

        def joined(parts):
            overall = parts[0][0]
            for part in parts[1:]:
                overall = jnp.maximum(overall, part[0])
            factors = [jnp.exp2((part[0] - overall) * scale) for part in parts]
            total = sum(f * part[1] for f, part in zip(factors, parts))
            acc = sum(f * part[2] for f, part in zip(factors, parts))
            return overall, total, acc

        def put(k, members_part, top, total, acc):
            first, count = k * members + members_part.start, members_part.stop - members_part.start
            osend[pl.ds(first, count)] = acc.astype(jnp.bfloat16).reshape(count, slice_rows, HEAD_WIDTH)
            for j in range(count):
                part = slice(j * slice_rows, (j + 1) * slice_rows)
                ssend[first + j] = jnp.concatenate([as_row(top[part]), as_row(total[part])], axis=0)

        def rows_of(members_part):
            return slice(members_part.start * slice_rows, members_part.stop * slice_rows)

        def prepare(k, members_part):
            rows = rows_of(members_part)
            top, total, weights = weigh(k, members_part, len(sure), late_blocks)
            late_top[rows] = jnp.broadcast_to(top, (weights.shape[0], HEAD_WIDTH))
            late_total[rows] = jnp.broadcast_to(total, (weights.shape[0], HEAD_WIDTH))
            late_weights[rows] = weights

        def finish(k, members_part):
            rows = rows_of(members_part)
            early = [ref[rows] for ref in (early_top, early_total, early_acc)]
            late = [late_top[rows], late_total[rows], summed(late_weights[rows], len(sure))]
            put(k, members_part, *joined([early, late]))

        def give(k, members_part):
            for j in range(members_part.start, members_part.stop):
                n = k * members + j
                device = where_is(2 * k + half, j)
                to_me = (kind == k) & (member == j)

                @pl.when(to_me)
                def _():
                    pltpu.make_async_copy(osend.at[n], obuf.at[core, kind, chip], o_recv.at[core]).start()
                    pltpu.make_async_copy(ssend.at[n], sbuf.at[core, kind, chip], s_recv.at[core]).start()

                @pl.when(jnp.logical_not(to_me))
                def _():
                    remote(ssend.at[n], sbuf.at[core, kind, chip], s_send, s_recv.at[core], device).start()
                    remote(osend.at[n], obuf.at[core, kind, chip], o_send, o_recv.at[core], device).start()

        begin(0)

        def wait_only(t):
            return lambda i, there, e: landed(t, i)

        pl.when(is_second)(lambda: mate_slots(hand_over(0)))
        pl.when(is_first)(lambda: mate_slots(wait_only(0)))

        prepare(0, everyone)

        pl.when(is_second)(lambda: mate_slots(hand_over(1), 1))
        pl.when(is_first)(lambda: mate_slots(wait_only(1), 1))

        for piece in pieces:
            finish(0, piece)
            give(0, piece)

        def attend(k):
            await_queries(k)
            put(k, everyone, *part_of(k, everyone, 0, own_blocks + late_blocks))
            give(k, everyone)

        if classes <= 4:
            for k in range(1, classes):
                attend(k)
        else:
            pl.loop(1, classes)(attend)

        @pl.when(i_am_live)
        def _():
            sent = kvbuf.at[:, pl.ds(0, chips + 1)]
            pltpu.make_async_copy(sent, sent, kv_send).wait()

        def handed_on(i, there, e):
            @pl.when(is_second & (chip != e // 2))
            def _():
                sent = kvbuf.at[:, pl.ds(0, 2)]
                pltpu.make_async_copy(sent, sent, pass_send.at[i]).wait()

        def handed_over(i, there, e):
            sent = kvbuf.at[:, i]
            pl.when(is_second)(pltpu.make_async_copy(sent, sent, pass_send.at[i]).wait)

        own_slots(handed_on)
        mate_slots(handed_over)
        for buffer, sem in ((qbuf, q_send), (osend, o_send), (ssend, s_send)):
            others = buffer.at[pl.ds(0, messages - 1)]
            pltpu.make_async_copy(others, others, sem).wait()

        def collect(c):
            pltpu.make_async_copy(sbuf.at[c], sbuf.at[c], s_recv.at[c]).wait()
            shares = []
            for n in range(chips):
                tops = [sbuf[c, g, n, 0:1] for g in range(classes)]
                overall = tops[0]
                for t in tops[1:]:
                    overall = jnp.maximum(overall, t)
                factors = [jnp.exp2((t - overall) * scale) for t in tops]
                weight = sum(f * sbuf[c, g, n, 1:2] for g, f in enumerate(factors))
                weight = jnp.where(weight > 0.0, weight, 1.0)
                shares.append([as_column(f / weight) for f in factors])
            pltpu.make_async_copy(obuf.at[c], obuf.at[c], o_recv.at[c]).wait()
            for n in range(chips):
                e = 2 * n + c
                wide[e] = sum(share * obuf[c, g, n].astype(jnp.float32) for g, share in enumerate(shares[n]))
                for h in range(heads):
                    first = (e * heads + h) * HEAD_WIDTH
                    out_ref[:, first:first + HEAD_WIDTH] = wide[e, h * local_rows:(h + 1) * local_rows].astype(out_ref.dtype)

        collect(1)
        collect(0)

    bf16, dma = jnp.bfloat16, pltpu.SemaphoreType.DMA
    signal = pltpu.SemaphoreType.REGULAR
    scratch = [
        pltpu.SMEM((blocks_n,), jnp.int32),
        pltpu.VMEM((local_rows, QUERY_HEADS * HEAD_WIDTH), bf16),
        pltpu.VMEM((2, BLOCK, KEY_VALUE_HEADS * HEAD_WIDTH), bf16),
        signal, signal,
        pltpu.VMEM((members, slice_rows, HEAD_WIDTH), bf16),
        pltpu.VMEM((members, slice_rows, HEAD_WIDTH), jnp.float32),
        pltpu.VMEM((messages, slice_rows, HEAD_WIDTH), bf16),
        pltpu.VMEM((2, slots_n, BLOCK, HEAD_WIDTH), bf16),
        pltpu.VMEM((chunk_rows, HEAD_WIDTH), jnp.float32),
        pltpu.VMEM((chunk_rows, HEAD_WIDTH), jnp.float32),
        pltpu.VMEM((chunk_rows, HEAD_WIDTH), jnp.float32),
        pltpu.VMEM((chunk_rows, HEAD_WIDTH), jnp.float32),
        pltpu.VMEM((chunk_rows, HEAD_WIDTH), jnp.float32),
        pltpu.VMEM((chunk_rows, (slots_n - len(sure)) * BLOCK), bf16),
        pltpu.VMEM((messages, slice_rows, HEAD_WIDTH), bf16),
        pltpu.VMEM((messages, 2, BLOCK), jnp.float32),
        pltpu.VMEM((2, classes, chips, slice_rows, HEAD_WIDTH), bf16),
        pltpu.VMEM((2, classes, chips, 2, BLOCK), jnp.float32),
        dma, dma((classes,)), dma, dma((2, slots_n)), dma((slots_n,)),
        dma, dma((2,)), dma, dma((2,)),
    ]
    return kernel, scratch


def solution(mesh):
    rows_n, cols_n = mesh.shape["qrow"], mesh.shape["kcol"]

    def per_device(queries, keys_values, doc_blocks):
        local_rows = queries.shape[0]
        kernel, scratch = make_kernel(rows_n, cols_n, queries.shape[0], doc_blocks.shape[0])
        merged = pl.pallas_call(
            kernel,
            out_shape=pltpu.VMEM(queries.shape, queries.dtype),
            in_specs=[
                pl.BlockSpec(memory_space=pl.ANY),
                pl.BlockSpec(memory_space=pl.ANY),
                pl.BlockSpec(memory_space=pl.ANY),
            ],
            out_specs=pl.BlockSpec(memory_space=pltpu.VMEM),
            scratch_shapes=scratch,
            compiler_params=pltpu.CompilerParams(collective_id=0, has_side_effects=True),
        )(doc_blocks, queries, keys_values)

        return merged

    return jax.shard_map(
        per_device,
        mesh=mesh,
        in_specs=(P(("qrow", "kcol"), None), P(None, ("kcol", "qrow"), None), P()),
        out_specs=P(("qrow", "kcol"), None),
        check_vma=False,
    )
```

```python
import math

import jax
import jax.numpy as jnp
from jax import lax
from jax.experimental import pallas as pl
from jax.experimental.pallas import tpu as pltpu
from jax.sharding import PartitionSpec as P

QUERY_HEADS = 64
KEY_VALUE_HEADS = 4
HEAD_WIDTH = 128
BLOCK = 128
MESH = pl.DeviceIdType.MESH

masked_score = -1e30


def dot(a, b, dims):
    return lax.dot_general(a, b, (dims, ((), ())), preferred_element_type=jnp.float32)


def make_kernel(rows_n, cols_n, local_rows, blocks_n):
    fold = max(1, 8 // cols_n)
    planes = rows_n // fold
    members = fold * cols_n
    chips = members // 2
    classes = planes // 2
    heads = QUERY_HEADS // members
    slice_rows = local_rows * heads
    chunk_rows = members * slice_rows
    devices = rows_n * cols_n
    total_queries = devices * local_rows
    query_blocks = total_queries // BLOCK
    stripe_blocks = blocks_n // query_blocks
    chunk_queries = members * local_rows
    messages = classes * members
    assert BLOCK % chunk_queries == 0 and blocks_n == devices and cols_n % 2 == 0 and 2 * slice_rows <= BLOCK
    assert planes % 2 == 0
    first_live = max(0, stripe_blocks - 1 - blocks_n // 2)
    block_of = lambda e, p: (e % cols_n) * rows_n + p * fold + e // cols_n
    alive = lambda e, half: [block_of(e, p) >= first_live for p in range(half, planes, 2)]
    sure = [e for e in range(members) if all(alive(e, 0) + alive(e, 1))]
    maybe = [(half, e) for half in range(2) for e in range(members) if e not in sure and any(alive(e, half))]
    spare = 2 * len(sure)
    slots_n = spare + len(maybe)
    scale = math.log2(math.e) / math.sqrt(HEAD_WIDTH)

    assert chips + 1 <= slots_n
    assert sure and chips & (chips - 1) == 0
    steps = sorted(range(1, chips), key=lambda k: (bin(k).count("1"), -k))

    routes = [steps, [*steps[1:], steps[0]]]

    def crossed(chip, k):
        bits = [1 << n for n in range(chips.bit_length() - 1) if k >> n & 1]
        return chip + sum(bit * (1 - 2 * (chip // bit % 2)) for bit in bits)

    def where_is(plane, member):
        return (plane * fold + member // cols_n, member % cols_n)

    def kernel(doc_any, q_any, kv_any, out_ref, doc_ref, q_ref, local, ready_sem,
               qsend, wide, qbuf, kvbuf, early_top, early_total, early_acc, late_top, late_total, late_weights, osend, ssend, obuf, sbuf,
               q_send, q_recv, kv_send, kv_recv, pass_send, o_send, o_recv, s_send, s_recv):
        row, col = lax.axis_index("qrow"), lax.axis_index("kcol")
        plane, core = row // fold, lax.rem(col, 2)
        member = (row % fold) * cols_n + col
        chip = member // 2
        half, kind = lax.rem(plane, 2), plane // 2
        mate = plane + 1 - 2 * half
        me = kind * members + member
        my_block = block_of(member, plane)
        partner = (row, col + 1 - 2 * core)
        mate_core = where_is(mate, chip * 2 + 1)
        is_first, is_second = core == 0, core == 1
        barrier = pltpu.get_barrier_semaphore()
        fetches = [pltpu.make_async_copy(kv_any.at[t], local.at[t], sem) for t, sem in enumerate((kv_send, s_send))]
        for fetch in fetches:
            fetch.start()

        def peer_plane(k):
            return lax.rem(kind + k, classes) * 2 + half

        def greet(plane_, member_):
            pl.semaphore_signal(barrier, inc=1, device_id=where_is(plane_, member_), device_id_type=MESH)

        for k in range(1, chips):
            greet(plane, lax.rem(chip + k, chips) * 2 + 1)
        pl.when(is_first)(lambda: greet(plane, chip * 2 + 1))
        for k in range(1, classes):
            for i in range(chips):
                greet(peer_plane(k), 2 * i)
        greet(mate, chip * 2)

        q_fetch = pltpu.make_async_copy(q_any, q_ref, q_send)
        q_fetch.start()
        doc_fetch = pltpu.make_async_copy(doc_any, doc_ref, o_send)
        doc_fetch.start()

        for i, (h, e) in enumerate(maybe):
            @pl.when(block_of(e, 2 * kind + h) < first_live)
            def _():
                kvbuf[:, spare + i] = jnp.zeros((2, BLOCK, HEAD_WIDTH), kvbuf.dtype)

        @pl.when(is_second)
        def _():
            pl.semaphore_wait(barrier, members - 1)
            pl.semaphore_signal(ready_sem, inc=1, device_id=partner, device_id_type=MESH)

        @pl.when(is_first)
        def _():
            pl.semaphore_wait(ready_sem, 1)

        def remote(src, dst, sent, got, device):
            return pltpu.make_async_remote_copy(
                src_ref=src, dst_ref=dst, send_sem=sent, recv_sem=got, device_id=device, device_id_type=MESH)

        is_sure = sum((member == e).astype(jnp.int32) for e in sure)
        my_slot = sum(i * (member == e).astype(jnp.int32) for i, e in enumerate(sure))
        my_slot = my_slot + sum((spare + i) * ((member == e) & (half == h)).astype(jnp.int32)
                                for i, (h, e) in enumerate(maybe))
        my_slot_there = my_slot + len(sure) * is_sure

        def kv_part(t, c):
            first = pl.multiple_of(2 * c * heads // (QUERY_HEADS // KEY_VALUE_HEADS) * HEAD_WIDTH, HEAD_WIDTH)
            return local.at[t, :, pl.ds(first, HEAD_WIDTH)]

        def kv_copy(t, k):
            other = crossed(chip, k)
            return remote(kv_part(t, other), kvbuf.at[t, my_slot], kv_send, kv_recv.at[t, my_slot],
                          where_is(plane, other * 2 + 1))

        def to_partner(t):
            return remote(kv_part(t, chip), kvbuf.at[t, my_slot], kv_send, kv_recv.at[t, my_slot], partner)

        def to_mate(t):
            return remote(kv_part(t, chip), kvbuf.at[t, my_slot_there], kv_send,
                          kv_recv.at[t, my_slot_there], mate_core)

        i_am_live = my_block >= first_live

        fetches[0].wait()

        @pl.when(i_am_live)
        def _():
            for k in routes[0]:
                kv_copy(0, k).start()

        fetches[1].wait()

        @pl.when(i_am_live)
        def _():
            for k in routes[1]:
                kv_copy(1, k).start()
            for t in range(2):
                pltpu.make_async_copy(kv_part(t, chip), kvbuf.at[t, my_slot], kv_recv.at[t, my_slot]).start()
                to_partner(t).start()

        q_fetch.wait()
        for e in range(members):
            for h in range(heads):
                first = (e * heads + h) * HEAD_WIDTH
                wide[e, h * local_rows:(h + 1) * local_rows] = q_ref[:, first:first + HEAD_WIDTH].astype(jnp.float32)
            qsend[e] = wide[e].astype(qsend.dtype)
        doc_fetch.wait()

        def q_copy(k, e):
            return remote(qsend.at[e], qbuf.at[me], q_send, q_recv.at[kind], where_is(peer_plane(k), e))

        def q_to(k, chips_crossed):
            for n in chips_crossed:
                for c in range(2):
                    if n == 0 and k == 0:
                        if c == 0:
                            q_copy(0, member + 1 - 2 * core).start()
                    else:
                        q_copy(k, crossed(chip, n) * 2 + c).start()

        near = [n for n in range(chips) if n % 2 == 0]
        far = [n for n in range(chips) if n % 2 == 1]

        keys_first = (is_sure == 1) & (kind > 0)

        def q_far():
            for k in [*range(1, classes), 0]:
                q_to(k, far)

        pltpu.make_async_copy(qsend.at[member], qbuf.at[me], q_recv.at[kind]).start()
        q_to(0, near)

        @pl.when(is_first)
        def _():
            pl.semaphore_wait(barrier, (classes - 1) * members + 2)
            pl.semaphore_signal(ready_sem, inc=1, device_id=partner, device_id_type=MESH)

        @pl.when(is_second)
        def _():
            pl.semaphore_wait(ready_sem, 1)

        @pl.when(i_am_live)
        def _():
            to_mate(0).start()
            to_mate(1).start()

        for k in range(1, classes):
            q_to(k, near)
        pl.when(jnp.logical_not(keys_first))(q_far)

        def landed(t, i):
            pltpu.make_async_copy(kvbuf.at[t, i], kvbuf.at[t, i], kv_recv.at[t, i]).wait()

        def to_first(t, i):
            return remote(kvbuf.at[t, i], kvbuf.at[t, i], pass_send.at[i], kv_recv.at[t, i], partner)

        def to_next(t, i, there):
            return remote(kvbuf.at[t, i], kvbuf.at[t, there], pass_send.at[i], kv_recv.at[t, there], mate_core)

        def in_order(of_half, first, step, t=0):
            def unsure(k):
                for n, (h, f) in enumerate(maybe):
                    is_live = (crossed(chip, k) == f // 2) & (of_half == h) & (block_of(f, 2 * kind + h) >= first_live)
                    pl.when(is_live)(lambda: step(spare + n, spare + n, f))

            if t == 1:
                for k in [0] + steps:
                    unsure(k)
            for k in [0] + routes[t]:
                for c in (1, 0):
                    e = crossed(chip, k) * 2 + c
                    i = sum(n * (e == f).astype(jnp.int32) for n, f in enumerate(sure))
                    found = sum((e == f).astype(jnp.int32) for f in sure) == 1
                    pl.when(found)(lambda: step(first + i, len(sure) + i, e))
                if t == 0:
                    unsure(k)

        def own_slots(step, t=0):
            in_order(half, 0, step, t)

        def mate_slots(step, t=0):
            in_order(1 - half, len(sure), step, t)

        def hand_on(t):
            def step(i, there, e):
                landed(t, i)

                @pl.when(is_second & (chip != e // 2))
                def _():
                    to_next(t, i, there).start()
                    to_first(t, i).start()
            return step

        def hand_over(t):
            def step(i, there, e):
                landed(t, i)
                to_first(t, i).start()
            return step

        own_slots(hand_on(0))
        pl.when(keys_first)(q_far)
        own_slots(hand_on(1), 1)

        lane = lax.broadcasted_iota(jnp.int32, (chunk_rows, BLOCK), 1)
        row_index = lax.broadcasted_iota(jnp.int32, (chunk_rows, BLOCK), 0)
        key_ahead = lane - (row_index // slice_rows * local_rows + row_index % local_rows)
        place = (lax.broadcasted_iota(jnp.int32, (slice_rows, BLOCK), 1)
                 == lax.broadcasted_iota(jnp.int32, (slice_rows, BLOCK), 0))
        as_row = lambda column: jnp.sum(jnp.where(place, column, 0.0), axis=0, keepdims=True)
        as_column = lambda row: jnp.sum(jnp.where(place, row, 0.0), axis=1, keepdims=True)

        def weigh(k, members_part, first_slot, blocks):
            first, count = k * members + members_part.start, members_part.stop - members_part.start
            rows = slice(members_part.start * slice_rows, members_part.stop * slice_rows)
            q = qbuf[pl.ds(first, count)].reshape(count * slice_rows, HEAD_WIDTH)
            query_first = (2 * k + half) * chunk_queries
            query_block = (query_first // BLOCK + 1) * stripe_blocks - 1
            ahead = key_ahead[rows] - query_first % BLOCK
            query_doc = doc_ref[query_block]
            held = slice(first_slot, first_slot + len(blocks))
            keys = kvbuf[0, held].reshape(len(blocks) * BLOCK, HEAD_WIDTH)
            scores = dot(q, keys, ((1,), (1,)))
            masked = []
            for i, b in enumerate(blocks):
                same = doc_ref[b] == query_doc
                reach = jnp.where(b < query_block, BLOCK, jnp.where(b == query_block, 0, -2 * BLOCK))
                reach = jnp.where(same, reach, -2 * BLOCK)
                masked.append(jnp.where(ahead <= reach, scores[:, i * BLOCK:(i + 1) * BLOCK], masked_score))
            top = masked[0]
            for s in masked[1:]:
                top = jnp.maximum(top, s)
            top = jnp.maximum(jnp.max(top, axis=1, keepdims=True), 0.5 * masked_score)
            weights = [jnp.exp2((s - top) * scale) for s in masked]
            total = weights[0]
            for p in weights[1:]:
                total = total + p
            total = jnp.sum(total, axis=1, keepdims=True)
            return top, total, jnp.concatenate([p.astype(jnp.bfloat16) for p in weights], axis=1)

        def summed(weights, first_slot):
            count = weights.shape[1] // BLOCK
            values = kvbuf[1, first_slot:first_slot + count].reshape(count * BLOCK, HEAD_WIDTH)
            return dot(weights, values, ((1,), (0,)))

        def part_of(k, members_part, first_slot, blocks):
            top, total, weights = weigh(k, members_part, first_slot, blocks)
            return top, total, summed(weights, first_slot)

        own_blocks = [block_of(e, plane) for e in sure]
        late_blocks = [block_of(e, mate) for e in sure] + [block_of(e, 2 * kind + h) for h, e in maybe]
        everyone = slice(0, members)
        pieces = [slice(0, members // 2), slice(members // 2, members)]

        def await_queries(k):
            mine = qbuf.at[pl.ds(k * members, members)]
            pltpu.make_async_copy(mine, mine, q_recv.at[k]).wait()

        def begin(k):
            await_queries(k)
            top, total, acc = part_of(k, everyone, 0, own_blocks)
            early_acc[...] = acc
            early_top[...] = jnp.broadcast_to(top, (chunk_rows, HEAD_WIDTH))
            early_total[...] = jnp.broadcast_to(total, (chunk_rows, HEAD_WIDTH))

        def joined(parts):
            overall = parts[0][0]
            for part in parts[1:]:
                overall = jnp.maximum(overall, part[0])
            factors = [jnp.exp2((part[0] - overall) * scale) for part in parts]
            total = sum(f * part[1] for f, part in zip(factors, parts))
            acc = sum(f * part[2] for f, part in zip(factors, parts))
            return overall, total, acc

        def put(k, members_part, top, total, acc):
            first, count = k * members + members_part.start, members_part.stop - members_part.start
            osend[pl.ds(first, count)] = acc.astype(jnp.bfloat16).reshape(count, slice_rows, HEAD_WIDTH)
            for j in range(count):
                part = slice(j * slice_rows, (j + 1) * slice_rows)
                ssend[first + j] = jnp.concatenate([as_row(top[part]), as_row(total[part])], axis=0)

        def rows_of(members_part):
            return slice(members_part.start * slice_rows, members_part.stop * slice_rows)

        def prepare(k, members_part):
            rows = rows_of(members_part)
            top, total, weights = weigh(k, members_part, len(sure), late_blocks)
            late_top[rows] = jnp.broadcast_to(top, (weights.shape[0], HEAD_WIDTH))
            late_total[rows] = jnp.broadcast_to(total, (weights.shape[0], HEAD_WIDTH))
            late_weights[rows] = weights

        def finish(k, members_part):
            rows = rows_of(members_part)
            early = [ref[rows] for ref in (early_top, early_total, early_acc)]
            late = [late_top[rows], late_total[rows], summed(late_weights[rows], len(sure))]
            put(k, members_part, *joined([early, late]))

        def give(k, members_part):
            for j in range(members_part.start, members_part.stop):
                n = k * members + j
                device = where_is(2 * k + half, j)
                to_me = (kind == k) & (member == j)

                @pl.when(to_me)
                def _():
                    pltpu.make_async_copy(osend.at[n], obuf.at[core, kind, chip], o_recv.at[core]).start()
                    pltpu.make_async_copy(ssend.at[n], sbuf.at[core, kind, chip], s_recv.at[core]).start()

                @pl.when(jnp.logical_not(to_me))
                def _():
                    remote(ssend.at[n], sbuf.at[core, kind, chip], s_send, s_recv.at[core], device).start()
                    remote(osend.at[n], obuf.at[core, kind, chip], o_send, o_recv.at[core], device).start()

        begin(0)

        def wait_only(t):
            return lambda i, there, e: landed(t, i)

        pl.when(is_second)(lambda: mate_slots(hand_over(0)))
        pl.when(is_first)(lambda: mate_slots(wait_only(0)))

        prepare(0, everyone)

        pl.when(is_second)(lambda: mate_slots(hand_over(1), 1))
        pl.when(is_first)(lambda: mate_slots(wait_only(1), 1))

        for piece in pieces:
            finish(0, piece)
            give(0, piece)

        def attend(k):
            await_queries(k)
            put(k, everyone, *part_of(k, everyone, 0, own_blocks + late_blocks))
            give(k, everyone)

        if classes <= 4:
            for k in range(1, classes):
                attend(k)
        else:
            pl.loop(1, classes)(attend)

        @pl.when(i_am_live)
        def _():
            sent = kvbuf.at[:, pl.ds(0, chips + 1)]
            pltpu.make_async_copy(sent, sent, kv_send).wait()

        def handed_on(i, there, e):
            @pl.when(is_second & (chip != e // 2))
            def _():
                sent = kvbuf.at[:, pl.ds(0, 2)]
                pltpu.make_async_copy(sent, sent, pass_send.at[i]).wait()

        def handed_over(i, there, e):
            sent = kvbuf.at[:, i]
            pl.when(is_second)(pltpu.make_async_copy(sent, sent, pass_send.at[i]).wait)

        own_slots(handed_on)
        mate_slots(handed_over)
        for buffer, sem in ((qbuf, q_send), (osend, o_send), (ssend, s_send)):
            others = buffer.at[pl.ds(0, messages - 1)]
            pltpu.make_async_copy(others, others, sem).wait()

        def collect(c):
            pltpu.make_async_copy(sbuf.at[c], sbuf.at[c], s_recv.at[c]).wait()
            shares = []
            for n in range(chips):
                tops = [sbuf[c, g, n, 0:1] for g in range(classes)]
                overall = tops[0]
                for t in tops[1:]:
                    overall = jnp.maximum(overall, t)
                factors = [jnp.exp2((t - overall) * scale) for t in tops]
                weight = sum(f * sbuf[c, g, n, 1:2] for g, f in enumerate(factors))
                weight = jnp.where(weight > 0.0, weight, 1.0)
                shares.append([as_column(f / weight) for f in factors])
            pltpu.make_async_copy(obuf.at[c], obuf.at[c], o_recv.at[c]).wait()
            for n in range(chips):
                e = 2 * n + c
                wide[e] = sum(share * obuf[c, g, n].astype(jnp.float32) for g, share in enumerate(shares[n]))
                for h in range(heads):
                    first = (e * heads + h) * HEAD_WIDTH
                    out_ref[:, first:first + HEAD_WIDTH] = wide[e, h * local_rows:(h + 1) * local_rows].astype(out_ref.dtype)

        collect(1)
        collect(0)

    bf16, dma = jnp.bfloat16, pltpu.SemaphoreType.DMA
    signal = pltpu.SemaphoreType.REGULAR
    scratch = [
        pltpu.SMEM((blocks_n,), jnp.int32),
        pltpu.VMEM((local_rows, QUERY_HEADS * HEAD_WIDTH), bf16),
        pltpu.VMEM((2, BLOCK, KEY_VALUE_HEADS * HEAD_WIDTH), bf16),
        signal,
        pltpu.VMEM((members, slice_rows, HEAD_WIDTH), bf16),
        pltpu.VMEM((members, slice_rows, HEAD_WIDTH), jnp.float32),
        pltpu.VMEM((messages, slice_rows, HEAD_WIDTH), bf16),
        pltpu.VMEM((2, slots_n, BLOCK, HEAD_WIDTH), bf16),
        pltpu.VMEM((chunk_rows, HEAD_WIDTH), jnp.float32),
        pltpu.VMEM((chunk_rows, HEAD_WIDTH), jnp.float32),
        pltpu.VMEM((chunk_rows, HEAD_WIDTH), jnp.float32),
        pltpu.VMEM((chunk_rows, HEAD_WIDTH), jnp.float32),
        pltpu.VMEM((chunk_rows, HEAD_WIDTH), jnp.float32),
        pltpu.VMEM((chunk_rows, (slots_n - len(sure)) * BLOCK), bf16),
        pltpu.VMEM((messages, slice_rows, HEAD_WIDTH), bf16),
        pltpu.VMEM((messages, 2, BLOCK), jnp.float32),
        pltpu.VMEM((2, classes, chips, slice_rows, HEAD_WIDTH), bf16),
        pltpu.VMEM((2, classes, chips, 2, BLOCK), jnp.float32),
        dma, dma((classes,)), dma, dma((2, slots_n)), dma((slots_n,)),
        dma, dma((2,)), dma, dma((2,)),
    ]
    return kernel, scratch


def solution(mesh):
    rows_n, cols_n = mesh.shape["qrow"], mesh.shape["kcol"]

    def per_device(queries, keys_values, doc_blocks):
        local_rows = queries.shape[0]
        kernel, scratch = make_kernel(rows_n, cols_n, queries.shape[0], doc_blocks.shape[0])
        merged = pl.pallas_call(
            kernel,
            out_shape=pltpu.VMEM(queries.shape, queries.dtype),
            in_specs=[
                pl.BlockSpec(memory_space=pl.ANY),
                pl.BlockSpec(memory_space=pl.ANY),
                pl.BlockSpec(memory_space=pl.ANY),
            ],
            out_specs=pl.BlockSpec(memory_space=pltpu.VMEM),
            scratch_shapes=scratch,
            compiler_params=pltpu.CompilerParams(collective_id=0, has_side_effects=True),
        )(doc_blocks, queries, keys_values)

        return merged

    return jax.shard_map(
        per_device,
        mesh=mesh,
        in_specs=(P(("qrow", "kcol"), None), P(None, ("kcol", "qrow"), None), P()),
        out_specs=P(("qrow", "kcol"), None),
        check_vma=False,
    )
```
